128 devices in a mesh: cluster: 8 (over x_hi, y), member: 16 (over z, x_lo, core).
Axes of the slice: x: 4 (x_hi: 2, x_lo: 2; x = x_hi * 2 + x_lo), y: 4, z: 4, core: 2. Of those that a mesh axis runs over, the one named last changes fastest.
Arguments:
- embeddings: bfloat16 [32768, 4096], P(('cluster', 'member')), may hold values from -15 to 15, as said below
- start_basis: bfloat16 [4096, 512], P(('cluster', 'member')), may hold values from -6 to 6
- cluster_ids: int32 [32768], P(('cluster', 'member')), may hold values from 0 to 7
- valid_counts: int32 [8], P('cluster'), may hold values from 1024 to 4096
Outputs:
- subspace: float32 [4096, 512], P(('cluster', 'member'))
- nearest: float32 [32768], P(('cluster', 'member'))
The draws below stay inside these ranges and needn't reach their ends.
Inputs may be any that keep to these rules, and one draw needn't show every extreme that they name: `embeddings`: Real-valued entries.
All inputs are finite; a program needn't handle non-finite values.
Results may differ from the reference program's by a relative error of at most 0.0042.
Values may be sent and summed in bfloat16 or wider, within the bound.
A program may use at most 64 MiB of HBM per device.

```python
import math
import jax
import jax.numpy as jnp
from jax import lax

D = 4096
K = 512
ITERS = 2
LABELS = 8
GROUP_ROWS = 4096
GROUPS = 8
ROWS = 32768


def draw_embeddings(key, part):
    first_key, second_key = jax.random.split(key, 2)
    jitter = jnp.clip(jax.random.normal(first_key, (ROWS, D), jnp.float32), -6.0, 6.0)
    common = jnp.clip(jax.random.normal(second_key, (D,), jnp.float32), -4.0, 4.0)
    rising = 0.2 + 0.4 * jnp.arange(ROWS, dtype=jnp.float32) / ROWS
    return (jitter + rising[:, None] * common[None, :]).astype(jnp.bfloat16)


def place_ends(values, own_key, low, top_value):
    longest = values.shape.index(max(values.shape))
    spots = []
    for shift in (0, 1):
        where = [jax.random.randint(jax.random.fold_in(own_key, axis), (), 0, length) for axis, length in enumerate(values.shape)]
        where[longest] = (where[longest] + shift) % values.shape[longest]
        spots.append(tuple(where))
    return values.at[spots[0]].set(low).at[spots[1]].set(top_value)


def block_levels(stream_key, extent, cuts, smallest, high):
    factor_of, own = 1.0, jax.random.fold_in(stream_key, 6)
    for dim, parts in cuts:
        steps = jnp.exp(jax.random.uniform(jax.random.fold_in(own, dim), (parts,), jnp.float32, smallest / len(cuts), high / len(cuts)))
        factor_of = factor_of * jnp.repeat(steps, extent[dim] // parts).reshape([-1 if axis == dim else 1 for axis in range(len(extent))])
    return factor_of


def normal_values(own_key, extent, deviation, most, pieces=(), kind=jnp.bfloat16):
    drawn = deviation * jax.random.normal(own_key, extent, jnp.float32)
    if pieces:
        drawn = drawn * block_levels(own_key, extent, pieces, -0.22, 0.18)
    return jnp.clip(drawn, -most, most).astype(kind)


def setup_inputs(seed: int = 0) -> dict:
    key_list = jax.random.split(jax.random.key(seed), 5)
    return {
        "embeddings": draw_embeddings(jax.random.fold_in(key_list[4], 71), 0),
        "start_basis": normal_values(key_list[1], (D, K), 1.0, 6.0, ((0, 128),)),
        "cluster_ids": place_ends(jax.random.randint(key_list[2], (ROWS,), 0, LABELS), jax.random.fold_in(key_list[2], 1), 0, LABELS - 1).astype(jnp.int32),
        "valid_counts": place_ends(jax.random.randint(key_list[3], (GROUPS,), GROUP_ROWS // 4, GROUP_ROWS + 1), jax.random.fold_in(key_list[3], 1), GROUP_ROWS // 4, GROUP_ROWS).astype(jnp.int32),
    }


EPS = 1e-06

def group_nearest(operands):
    units, labels, limit = operands
    scores = jnp.dot(units.astype(jnp.float32), units.T.astype(jnp.float32), preferred_element_type=jnp.float32)
    position = jnp.arange(units.shape[0], dtype=jnp.int32)
    allowed = (labels[:, None] == labels[None, :]) & (position[None, :] < limit) & (position[None, :] != position[:, None])
    return lax.optimization_barrier(jnp.max(jnp.where(allowed, scores, -1.0), axis=1))

def reference(embeddings, start_basis, cluster_ids, valid_counts):
    total_rows = embeddings.shape[0]
    average = lax.optimization_barrier(jnp.sum(embeddings.astype(jnp.float32), axis=0)) / total_rows
    centered = (embeddings.astype(jnp.float32) - average).astype(jnp.bfloat16)
    basis = start_basis
    orthonormal = None
    for sweep in range(ITERS):
        projected = jnp.dot(centered.astype(jnp.float32), basis.astype(jnp.float32), preferred_element_type=jnp.float32).astype(jnp.bfloat16)
        image = jnp.dot(centered.T.astype(jnp.float32), projected.astype(jnp.float32), preferred_element_type=jnp.float32) / total_rows
        gram = jnp.dot(image.T, image, precision=lax.Precision.HIGHEST)
        lower = jnp.linalg.cholesky(gram)
        orthonormal = jax.scipy.linalg.solve_triangular(lower, image.T, lower=True).T
        basis = orthonormal.astype(jnp.bfloat16)
    subspace = orthonormal * math.sqrt(D)
    coords = jnp.dot(centered.astype(jnp.float32), basis.astype(jnp.float32), preferred_element_type=jnp.float32)
    unit = (coords * lax.rsqrt(lax.optimization_barrier(jnp.sum(coords * coords, axis=1, keepdims=True)) + EPS)).astype(jnp.bfloat16)
    grouped_units = unit.reshape(GROUPS, GROUP_ROWS, K)
    grouped_labels = cluster_ids.reshape(GROUPS, GROUP_ROWS)
    nearest = lax.map(group_nearest, (grouped_units, grouped_labels, valid_counts))
    return (subspace, nearest.reshape(-1))
```

```python
import functools
import math

import jax
import jax.numpy as jnp
import numpy as np
from jax import lax
from jax.experimental import pallas as pl
from jax.experimental.pallas import tpu as pltpu
from jax.sharding import PartitionSpec as P

EPS = 1e-06
MESH = pl.DeviceIdType.MESH
F32 = jnp.float32
BF16 = jnp.bfloat16
D = 4096
K = 512
ROWS = 32768
VMEM_LIMIT = 60 * 1024 * 1024


class Links:
    def __init__(self, send, recv):
        self.send, self.recv, self.used = send, recv, 0

    def slot(self):
        self.used += 1
        return self.used - 1

    def copy(self, slot, src, dst, device):
        return pltpu.make_async_remote_copy(
            src_ref=src,
            dst_ref=dst,
            send_sem=self.send.at[slot],
            recv_sem=self.recv.at[slot],
            device_id=device,
            device_id_type=MESH,
        )

    def arrived(self, slot, dst, device):
        self.copy(slot, dst, dst, device).wait_recv()


class Place:
    def __init__(self):
        c, m = lax.axis_index("cluster"), lax.axis_index("member")
        self.x = (c // 4) * 2 + (m // 2) % 2
        self.y = c % 4
        self.z = m // 4
        self.k = m % 2
        k, o = self.k, 1 - self.k
        self.coord = {
            "u": self.x * o + self.y * k,
            "v": self.y * o + self.z * k,
            "w": self.z * o + self.x * k,
        }

    def at(self, dx, dy, dz, core):
        x = (self.x + dx + 4) % 4
        y = (self.y + dy + 4) % 4
        z = (self.z + dz + 4) % 4
        return ((x // 2) * 4 + y, z * 4 + (x % 2) * 2 + core)

    def along(self, axis, d):
        k, o = self.k, 1 - self.k
        if axis == "u":
            return self.at(d * o, d * k, 0, k)
        if axis == "v":
            return self.at(0, d * o, d * k, k)
        return self.at(d * k, 0, d * o, k)

    def partner(self):
        return self.at(0, 0, 0, 1 - self.k)


def greet(devices):
    barrier = pltpu.get_barrier_semaphore()
    for device in devices:
        pl.semaphore_signal(barrier, inc=1, device_id=device, device_id_type=MESH)
    pl.semaphore_wait(barrier, len(devices))


def mo(i, n):
    return pl.multiple_of(i, n)


class GatherStage:
    def __init__(self, links, place, axis, buf, base, n, source=None):
        self.links, self.buf, self.n, self.h = links, buf, n, n // 2
        self.base, self.coord = base, place.coord[axis]
        self.plus, self.minus = place.along(axis, 1), place.along(axis, -1)
        self.slots = [links.slot() for _ in range(4)]
        self.source = source
        self.sent = []

    def region(self, d, part=None):
        start = mo(self.base + ((self.coord + d + 4) % 4) * self.n, self.n)
        if part is None:
            return self.buf.at[pl.ds(start, self.n)]
        return self.buf.at[pl.ds(mo(start + part * self.h, self.h), self.h)]

    def _send(self, i, src, dst, device):
        copy = self.links.copy(self.slots[i], src, dst, device)
        copy.start()
        self.sent.append(copy)

    def start(self):
        own = self.region(0)
        src = own if self.source is None else self.source
        self._send(0, src, own, self.plus)
        self._send(1, src, own, self.minus)

    def relay(self):
        self.links.arrived(self.slots[0], self.region(-1), self.plus)
        first = self.region(-1, 0)
        self._send(2, first, first, self.plus)
        self.links.arrived(self.slots[1], self.region(1), self.plus)
        second = self.region(1, 1)
        self._send(3, second, second, self.minus)

    def finish(self):
        self.links.arrived(self.slots[2], self.region(2, 0), self.plus)
        self.links.arrived(self.slots[3], self.region(2, 1), self.plus)
        for copy in self.sent:
            copy.wait_send()


def rows_loop(total, step, fn):
    if total <= step:
        fn(0, total)
        return

    def body(i, carry):
        fn(mo(i * step, step), step)
        return carry

    lax.fori_loop(0, total // step, body, 0)


def scatter_stage(links, place, axis, slab, n, dtype, bufs, out):
    h = n // 2
    s2, sp, sm, ra, rb, rp, rm = bufs
    plus, minus = place.along(axis, 1), place.along(axis, -1)
    slots = [links.slot() for _ in range(6)]
    sent = []
    cut = min(n, 128)
    hcut = min(h, 128)

    def send(i, src, dst, device):
        copy = links.copy(slots[i], src, dst, device)
        copy.start()
        sent.append(copy)

    term = slab(2)
    rows_loop(n, cut, lambda r, m: s2.__setitem__((pl.ds(r, m), slice(None)), term[pl.ds(r, m), :].astype(dtype)))
    send(0, s2.at[pl.ds(0, h)], ra, plus)
    send(1, s2.at[pl.ds(h, h)], rb, minus)
    ahead = slab(1)
    rows_loop(h, hcut, lambda r, m: sp.__setitem__((pl.ds(h + r, m), slice(None)), ahead[pl.ds(h + r, m), :].astype(dtype)))
    send(2, sp.at[pl.ds(h, h)], rp.at[pl.ds(h, h)], plus)
    behind = slab(-1)
    rows_loop(h, hcut, lambda r, m: sm.__setitem__((pl.ds(r, m), slice(None)), behind[pl.ds(r, m), :].astype(dtype)))
    send(3, sm.at[pl.ds(0, h)], rm.at[pl.ds(0, h)], minus)
    links.arrived(slots[0], ra, plus)
    rows_loop(
        h,
        hcut,
        lambda r, m: sp.__setitem__(
            (pl.ds(r, m), slice(None)),
            (ahead[pl.ds(r, m), :] + ra[pl.ds(r, m), :].astype(F32)).astype(dtype),
        ),
    )
    send(4, sp.at[pl.ds(0, h)], rp.at[pl.ds(0, h)], plus)
    links.arrived(slots[1], rb, plus)
    rows_loop(
        h,
        hcut,
        lambda r, m: sm.__setitem__(
            (pl.ds(h + r, m), slice(None)),
            (behind[pl.ds(h + r, m), :] + rb[pl.ds(r, m), :].astype(F32)).astype(dtype),
        ),
    )
    send(5, sm.at[pl.ds(h, h)], rm.at[pl.ds(h, h)], minus)
    own = slab(0)
    links.arrived(slots[2], rp.at[pl.ds(h, h)], plus)
    links.arrived(slots[3], rm.at[pl.ds(0, h)], plus)
    links.arrived(slots[4], rp.at[pl.ds(0, h)], plus)
    links.arrived(slots[5], rm.at[pl.ds(h, h)], plus)
    rows_loop(
        n,
        cut,
        lambda r, m: out.__setitem__(
            (pl.ds(r, m), slice(None)),
            own[pl.ds(r, m), :] + (rp[pl.ds(r, m), :].astype(F32) + rm[pl.ds(r, m), :].astype(F32)),
        ),
    )
    for copy in sent:
        copy.wait_send()


def stage_bufs(n, dtype):
    h = n // 2
    shapes = [(n, K), (n, K), (n, K), (h, K), (h, K), (n, K), (n, K)]
    return [pltpu.VMEM(shape, dtype) for shape in shapes]


STEP_SCRATCH = [
    pltpu.VMEM((2048, 1024), BF16),
    pltpu.VMEM((4, 512, K), F32),
    pltpu.VMEM((512, K), F32),
    pltpu.VMEM((128, K), F32),
    pltpu.VMEM((32, K), F32),
    pltpu.VMEM((512, 1024), F32),
    pltpu.VMEM((512, 1024), F32),
    pltpu.VMEM((1024, K), F32),
    pltpu.VMEM((1024, K), F32),
    *stage_bufs(512, BF16),
    *stage_bufs(128, F32),
    *stage_bufs(32, F32),
]


def power_step(links, place, xf, xt, proj, z_ref, g_ref, y_ref, scratch):
    yb, img, t1, t2, t3, za, ga, mine, theirs = scratch[:9]
    bufs = [scratch[9 + 7 * i : 16 + 7 * i] for i in range(3)]
    u, v, w = (place.coord[a] for a in "uvw")

    def image_slab(d):
        dst = img.at[d % 4]
        start = ((u + d + 4) % 4) * 512

        def part(r, m):
            dst[pl.ds(r, m), :] = jnp.dot(
                xt[pl.ds(mo(start + r, 128), m), :], proj[...], preferred_element_type=F32
            )

        rows_loop(512, 128, part)
        return dst

    scatter_stage(links, place, "u", image_slab, 512, BF16, bufs[0], t1)
    scatter_stage(
        links, place, "v", lambda d: t1.at[pl.ds(mo(((v + d + 4) % 4) * 128, 128), 128)], 128, F32, bufs[1], t2
    )
    scatter_stage(
        links, place, "w", lambda d: t2.at[pl.ds(mo(((w + d + 4) % 4) * 32, 32), 32)], 32, F32, bufs[2], t3
    )
    image = t3[...] * (1.0 / ROWS)
    high = image.astype(BF16)
    y_ref[:, 0:K] = high
    y_ref[:, K : 2 * K] = (image - high.astype(F32)).astype(BF16)
    own = mo((u * 16 + v * 4 + w) * 32, 32)
    yb[pl.ds(own, 32), :] = y_ref[...]
    for axis, base, n in (("w", (u * 16 + v * 4) * 32, 32), ("v", u * 512, 128)):
        stage = GatherStage(links, place, axis, yb, base, n, source=y_ref if axis == "w" else None)
        stage.start()
        stage.relay()
        stage.finish()

    def consume(d, first=False):
        start = ((u + d + 4) % 4) * 512
        rows = pl.ds(mo(start, 512), 512)

        def product(r, m):
            term = jnp.dot(xf[pl.ds(r, m), pl.ds(mo(start, 512), 512)], yb[rows, :], preferred_element_type=F32)
            za[pl.ds(r, m), :] = term if first else za[pl.ds(r, m), :] + term

        rows_loop(512, 128, product)

        def gram(r, m):
            term = lax.dot_general(
                yb[rows, pl.ds(r, m)], yb[rows, :], (((0,), (0,)), ((), ())), preferred_element_type=F32
            )
            ga[pl.ds(r, m), :] = term if first else ga[pl.ds(r, m), :] + term

        rows_loop(512, 128, gram)

    last = GatherStage(links, place, "u", yb, 0, 512)
    last.start()
    consume(0, first=True)
    last.relay()
    consume(1)
    consume(-1)
    last.finish()
    consume(2)
    mine[0:512, :] = za[:, 0:K] + za[:, K : 2 * K]
    cross = ga[:, K : 2 * K]
    mine[512:1024, :] = ga[:, 0:K] + (cross + cross.T)
    swap = links.copy(links.slot(), mine, theirs, place.partner())
    swap.start()
    swap.wait()
    z_ref[...] = mine[0:512, :] + theirs[0:512, :]
    g_ref[...] = mine[512:1024, :] + theirs[512:1024, :]


FIRST_SLOTS = 80


def first_kernel(
    e_ref, sb_ref, s0_ref, s1_ref, lab_ref,
    xf, xt, z_ref, g_ref, y_ref, labs_ref,
    send, recv, packed, xr, b0, sums, pa, pb, proj, *scratch,
):
    links, place = Links(send, recv), Place()
    u, v, w, k = (*(place.coord[a] for a in "uvw"), place.k)
    partner = place.partner()
    greet([place.along(a, d) for a in "uvw" for d in (1, -1, 2)] + [partner])
    own = mo((u * 16 + v * 4 + w) * 32, 32)
    g1 = GatherStage(links, place, "w", b0, (u * 16 + v * 4) * 32, 32, source=sb_ref)
    g1.start()
    b0[pl.ds(own, 32), :] = sb_ref[...]
    swap_labels = links.copy(links.slot(), lab_ref, labs_ref.at[pl.ds(mo(k * 256, 256), 256)], partner)
    swap_labels.start()
    labs_ref[pl.ds(mo(k * 256, 256), 256), :] = lab_ref[...]

    def pack(t, carry):
        x, y = t // 4, t % 4
        src = mo(((x // 2) * 4 + y) * 512, 512)
        packed[0, :, pl.ds(mo(t * 128, 128), 128)] = jnp.dot(
            e_ref[:, pl.ds(src, 512)], s0_ref[x % 2], preferred_element_type=F32
        ).astype(BF16)
        near = jnp.dot(e_ref[:, pl.ds(mo(t * 128, 128), 128)], s1_ref[0], preferred_element_type=F32)
        far = jnp.dot(e_ref[:, pl.ds(mo(2048 + t * 128, 128), 128)], s1_ref[1], preferred_element_type=F32)
        packed[1, :, pl.ds(mo(t * 128, 128), 128)] = (near + far).astype(BF16)
        return carry

    lax.fori_loop(0, 16, pack, 0)
    swap_rows = links.copy(links.slot(), packed.at[1 - k], xr.at[pl.ds(mo(k * 256, 256), 256)], partner)
    swap_rows.start()
    xr[pl.ds(mo(k * 256, 256), 256), :] = packed[k]
    g1.relay()
    g1.finish()
    g2 = GatherStage(links, place, "v", b0, u * 512, 128)
    g2.start()
    swap_rows.wait()

    def exchange(stage, axis, value):
        here = place.coord[axis]
        sums[stage, here] = value
        copies = []
        for d in (1, -1, 2):
            copy = links.copy(links.slot(), sums.at[stage, here], sums.at[stage, here], place.along(axis, d))
            copy.start()
            copies.append((copy, d))

        def done():
            for copy, _ in copies:
                copy.wait()
            return (sums[stage, 0] + sums[stage, 1]) + (sums[stage, 2] + sums[stage, 3])

        return done

    ones = jnp.ones((8, 512), BF16)
    done = exchange(0, "u", jnp.dot(ones, xr[...], preferred_element_type=F32))
    g2.relay()
    done = exchange(1, "v", done())
    g2.finish()
    g3 = GatherStage(links, place, "u", b0, 0, 512)
    g3.start()
    done = exchange(2, "w", done())
    average = done()[0:1, :] / ROWS
    g3.relay()

    def center(r, m):
        xf[pl.ds(r, m), :] = (xr[pl.ds(r, m), :].astype(F32) - average).astype(BF16)

    rows_loop(512, 32, center)

    def turn(t, carry):
        lanes = pl.ds(mo(t * 128, 128), 128)
        xt[lanes, :] = xf[:, lanes].T
        return carry

    lax.fori_loop(0, 16, turn, 0)
    g3.finish()

    def product(r, m):
        pa[pl.ds(r, m), :] = jnp.dot(xf[pl.ds(r, m), :], b0[...], preferred_element_type=F32)

    rows_loop(512, 128, product)
    swap = links.copy(links.slot(), pa, pb, partner)
    swap.start()
    swap_labels.wait()
    swap.wait()

    def total(r, m):
        proj[pl.ds(r, m), :] = (pa[pl.ds(r, m), :] + pb[pl.ds(r, m), :]).astype(BF16)

    rows_loop(512, 128, total)
    power_step(links, place, xf, xt, proj, z_ref, g_ref, y_ref, scratch)


def next_kernel(xf, xt, proj, z_ref, g_ref, y_ref, send, recv, *scratch):
    links, place = Links(send, recv), Place()
    greet([place.along(a, d) for a in "uvw" for d in (1, -1)] + [place.partner()])
    power_step(links, place, xf, xt, proj, z_ref, g_ref, y_ref, scratch)


def nearest_kernel(units, own_labels, labs, limit, out, send, recv, ub, best, theirs):
    links, place = Links(send, recv), Place()
    z, k, xl = place.z, place.k, place.x % 2
    flip = 1 - 2 * xl
    across = place.at(flip, 0, 0, k)
    up, down = place.at(0, 0, 1, k), place.at(0, 0, -1, k)
    partner = place.partner()
    greet([across, up, down, partner])
    own = ub.at[z, xl]
    own[0:256, :] = units[pl.ds(mo(k * 256, 256), 256), :]
    own[256:272, :] = own_labels[...]
    slots = [links.slot() for _ in range(8)]

    def zed(d):
        return (z + d + 4) % 4

    def send_all(pairs):
        copies = [links.copy(slots[i], ref, ref, device) for i, ref, device in pairs]
        for copy in copies:
            copy.start()
        return copies

    def got(i, ref):
        links.arrived(slots[i], ref, partner)

    @pl.when(k == 0)
    def _():
        sent = send_all([(0, own, across)])
        got(0, ub.at[z, 1 - xl])
        sent += send_all([(1, ub.at[z], up), (2, ub.at[z], down)])
        got(1, ub.at[zed(-1)])
        sent += send_all([(3, ub.at[zed(-1), 0], up)])
        got(2, ub.at[zed(1)])
        sent += send_all([(4, ub.at[zed(1), 1], down)])
        got(3, ub.at[zed(2), 0])
        got(4, ub.at[zed(2), 1])
        for copy in sent:
            copy.wait_send()

    @pl.when(k == 1)
    def _():
        sent = send_all([(0, own, across), (1, own, up), (2, own, down)])
        got(1, ub.at[zed(-1), xl])
        low = ub.at[zed(-1), xl, pl.ds(0, 144)]
        sent += send_all([(3, low, up), (5, ub.at[zed(-1), xl], across)])
        got(2, ub.at[zed(1), xl])
        high = ub.at[zed(1), xl, pl.ds(144, 128)]
        sent += send_all([(4, high, down), (6, ub.at[zed(1), xl], across)])
        got(3, ub.at[zed(2), xl, pl.ds(0, 144)])
        got(4, ub.at[zed(2), xl, pl.ds(144, 128)])
        sent += send_all([(7, ub.at[zed(2), xl], across)])
        got(0, ub.at[z, 1 - xl])
        got(5, ub.at[zed(-1), 1 - xl])
        got(6, ub.at[zed(1), 1 - xl])
        got(7, ub.at[zed(2), 1 - xl])
        for copy in sent:
            copy.wait_send()

    best[...] = jnp.full((512, 128), -1.0, F32)
    bound = limit[0:1, :]
    lane = lax.broadcasted_iota(jnp.int32, (1, 128), 1)
    mine_first = (z * 4 + xl * 2) * 256

    def block(b, carry):
        zz, xx = b // 2, b % 2
        labels = ub[zz, xx, 256:272, :][0:1, :].astype(F32)
        first = (zz * 4 + xx * 2 + k) * 256

        def part(r, m):
            score = lax.dot_general(
                units[pl.ds(r, m), :], ub[zz, xx, 0:256, :], (((1,), (1,)), ((), ())), preferred_element_type=F32
            )
            rows = lax.broadcasted_iota(jnp.int32, (m, 128), 0) + (mine_first + r)
            label = labs[pl.ds(r, m), :].astype(F32)
            top = best[pl.ds(r, m), :]
            for t in range(2):
                other = lane + (first + t * 128)
                use = (label == labels[:, t * 128 : t * 128 + 128]) & (other < bound) & (other != rows)
                top = jnp.maximum(top, jnp.where(use, score[:, t * 128 : t * 128 + 128], -1.0))
            best[pl.ds(r, m), :] = top

        rows_loop(512, 128, part)
        return carry

    lax.fori_loop(0, 8, block, 0)
    best[...] = jnp.broadcast_to(jnp.max(best[...], axis=1, keepdims=True), (512, 128))
    swap = links.copy(
        links.slot(), best.at[pl.ds(mo((1 - k) * 256, 256), 256)], theirs, partner
    )
    swap.start()
    swap.wait()
    out[...] = jnp.maximum(best[pl.ds(mo(k * 256, 256), 256), :], theirs[...])


def comm_call(kernel, outs, scratch, cid, slots, name):
    vmem = pl.BlockSpec(memory_space=pltpu.VMEM)

    def call(*args):
        return pl.pallas_call(
            kernel,
            out_shape=outs,
            in_specs=[vmem] * len(args),
            out_specs=jax.tree.map(lambda _: vmem, outs),
            scratch_shapes=[pltpu.SemaphoreType.DMA((slots,)), pltpu.SemaphoreType.DMA((slots,)), *scratch],
            compiler_params=pltpu.CompilerParams(
                collective_id=cid, has_side_effects=True, vmem_limit_bytes=VMEM_LIMIT
            ),
            name=name,
        )(*args)

    return call


def selections():
    s0 = np.zeros((2, 512, 128), np.float32)
    s1 = np.zeros((2, 128, 128), np.float32)
    r = np.arange(32)
    for lo in range(2):
        for z in range(4):
            s0[lo, z * 128 + lo * 64 + r, z * 32 + r] = 1
        for hi in range(2):
            s1[hi, (lo * 2 + 1) * 32 + r, (hi * 2 + lo) * 32 + r] = 1
    return jnp.asarray(s0, BF16), jnp.asarray(s1, BF16)


HIGH = lax.Precision.HIGHEST


def body(embeddings, start_basis, cluster_ids, valid_counts):
    step_out = [
        jax.ShapeDtypeStruct((512, K), F32),
        jax.ShapeDtypeStruct((K, K), F32),
        jax.ShapeDtypeStruct((32, 2 * K), BF16),
    ]
    x_out = [jax.ShapeDtypeStruct((512, 2048), BF16), jax.ShapeDtypeStruct((2048, 512), BF16)]
    labels = cluster_ids.astype(BF16)
    label_columns = jnp.broadcast_to(labels[:, None], (256, 128))
    s0, s1 = selections()
    xf, xt, z, gram, image, labs = comm_call(
        first_kernel,
        [*x_out, *step_out, jax.ShapeDtypeStruct((512, 128), BF16)],
        [
            pltpu.VMEM((2, 256, 2048), BF16),
            pltpu.VMEM((512, 2048), BF16),
            pltpu.VMEM((2048, K), BF16),
            pltpu.VMEM((3, 4, 8, 2048), F32),
            pltpu.VMEM((512, K), F32),
            pltpu.VMEM((512, K), F32),
            pltpu.VMEM((512, K), BF16),
            *STEP_SCRATCH,
        ],
        0,
        FIRST_SLOTS,
        "first_step",
    )(embeddings, start_basis, s0, s1, label_columns)

    def inverse_factor(gram):
        lower = jnp.linalg.cholesky(gram)
        return jax.scipy.linalg.solve_triangular(lower, jnp.eye(K, dtype=F32), lower=True)

    inverse = inverse_factor(gram)
    proj = jnp.dot(z, inverse.T, precision=HIGH).astype(BF16)
    z, gram, image = comm_call(next_kernel, step_out, STEP_SCRATCH, 1, FIRST_SLOTS, "next_step")(xf, xt, proj)
    inverse = inverse_factor(gram)
    own_image = image[:, :K].astype(F32) + image[:, K:].astype(F32)
    subspace = jnp.dot(own_image, inverse.T, precision=HIGH) * math.sqrt(D)
    coords = jnp.dot(z, inverse.T, precision=HIGH)
    unit = (coords * lax.rsqrt(jnp.sum(coords * coords, axis=1, keepdims=True) + EPS)).astype(BF16)
    limit = jnp.broadcast_to(valid_counts[None, :], (8, 128))
    own_labels = jnp.broadcast_to(jnp.concatenate([labels, labels])[None, :], (16, 512))
    nearest = comm_call(
        nearest_kernel,
        jax.ShapeDtypeStruct((256, 128), F32),
        [
            pltpu.VMEM((4, 2, 272, K), BF16),
            pltpu.VMEM((512, 128), F32),
            pltpu.VMEM((256, 128), F32),
        ],
        2,
        16,
        "nearest",
    )(unit, own_labels, labs, limit)
    return (subspace, nearest[:, 0])


def solution(mesh):
    placed = (
        P(("cluster", "member"), None),
        P(("cluster", "member"), None),
        P(("cluster", "member")),
        P("cluster"),
    )
    return jax.shard_map(
        body,
        mesh=mesh,
        in_specs=placed,
        out_specs=(P(("cluster", "member"), None), P(("cluster", "member"))),
        check_vma=False,
    )
```

```python
import functools
import math

import jax
import jax.numpy as jnp
import numpy as np
from jax import lax
from jax.experimental import pallas as pl
from jax.experimental.pallas import tpu as pltpu
from jax.sharding import PartitionSpec as P

EPS = 1e-06
MESH = pl.DeviceIdType.MESH
F32 = jnp.float32
BF16 = jnp.bfloat16
D = 4096
K = 512
ROWS = 32768
VMEM_LIMIT = 60 * 1024 * 1024


class Links:
    def __init__(self, send, recv):
        self.send, self.recv, self.used = send, recv, 0

    def slot(self):
        self.used += 1
        return self.used - 1

    def copy(self, slot, src, dst, device):
        return pltpu.make_async_remote_copy(
            src_ref=src,
            dst_ref=dst,
            send_sem=self.send.at[slot],
            recv_sem=self.recv.at[slot],
            device_id=device,
            device_id_type=MESH,
        )

    def arrived(self, slot, dst, device):
        self.copy(slot, dst, dst, device).wait_recv()


class Place:
    def __init__(self):
        c, m = lax.axis_index("cluster"), lax.axis_index("member")
        self.x = (c // 4) * 2 + (m // 2) % 2
        self.y = c % 4
        self.z = m // 4
        self.k = m % 2
        k, o = self.k, 1 - self.k
        self.coord = {
            "u": self.x * o + self.y * k,
            "v": self.y * o + self.z * k,
            "w": self.z * o + self.x * k,
        }

    def at(self, dx, dy, dz, core):
        x = (self.x + dx + 4) % 4
        y = (self.y + dy + 4) % 4
        z = (self.z + dz + 4) % 4
        return ((x // 2) * 4 + y, z * 4 + (x % 2) * 2 + core)

    def along(self, axis, d):
        k, o = self.k, 1 - self.k
        if axis == "u":
            return self.at(d * o, d * k, 0, k)
        if axis == "v":
            return self.at(0, d * o, d * k, k)
        return self.at(d * k, 0, d * o, k)

    def partner(self):
        return self.at(0, 0, 0, 1 - self.k)


def greet(devices):
    barrier = pltpu.get_barrier_semaphore()
    for device in devices:
        pl.semaphore_signal(barrier, inc=1, device_id=device, device_id_type=MESH)
    pl.semaphore_wait(barrier, len(devices))


def mo(i, n):
    return pl.multiple_of(i, n)


class GatherStage:
    def __init__(self, links, place, axis, buf, base, n, source=None):
        self.links, self.buf, self.n, self.h = links, buf, n, n // 2
        self.base, self.coord = base, place.coord[axis]
        self.plus, self.minus = place.along(axis, 1), place.along(axis, -1)
        self.slots = [links.slot() for _ in range(4)]
        self.source = source
        self.sent = []

    def region(self, d, part=None):
        start = mo(self.base + ((self.coord + d + 4) % 4) * self.n, self.n)
        if part is None:
            return self.buf.at[pl.ds(start, self.n)]
        return self.buf.at[pl.ds(mo(start + part * self.h, self.h), self.h)]

    def _send(self, i, src, dst, device):
        copy = self.links.copy(self.slots[i], src, dst, device)
        copy.start()
        self.sent.append(copy)

    def start(self):
        own = self.region(0)
        src = own if self.source is None else self.source
        self._send(0, src, own, self.plus)
        self._send(1, src, own, self.minus)

    def relay(self):
        self.links.arrived(self.slots[0], self.region(-1), self.plus)
        first = self.region(-1, 0)
        self._send(2, first, first, self.plus)
        self.links.arrived(self.slots[1], self.region(1), self.plus)
        second = self.region(1, 1)
        self._send(3, second, second, self.minus)

    def finish(self):
        self.links.arrived(self.slots[2], self.region(2, 0), self.plus)
        self.links.arrived(self.slots[3], self.region(2, 1), self.plus)
        for copy in self.sent:
            copy.wait_send()


def rows_loop(total, step, fn):
    if total <= step:
        fn(0, total)
        return

    def body(i, carry):
        fn(mo(i * step, step), step)
        return carry

    lax.fori_loop(0, total // step, body, 0)


def scatter_stage(links, place, axis, slab, n, dtype, bufs, out):
    h = n // 2
    s2, sp, sm, ra, rb, rp, rm = bufs
    plus, minus = place.along(axis, 1), place.along(axis, -1)
    slots = [links.slot() for _ in range(6)]
    sent = []
    cut = min(n, 128)
    hcut = min(h, 128)

    def send(i, src, dst, device):
        copy = links.copy(slots[i], src, dst, device)
        copy.start()
        sent.append(copy)

    term = slab(2)
    rows_loop(n, cut, lambda r, m: s2.__setitem__((pl.ds(r, m), slice(None)), term[pl.ds(r, m), :].astype(dtype)))
    send(0, s2.at[pl.ds(0, h)], ra, plus)
    send(1, s2.at[pl.ds(h, h)], rb, minus)
    ahead = slab(1)
    rows_loop(h, hcut, lambda r, m: sp.__setitem__((pl.ds(h + r, m), slice(None)), ahead[pl.ds(h + r, m), :].astype(dtype)))
    send(2, sp.at[pl.ds(h, h)], rp.at[pl.ds(h, h)], plus)
    behind = slab(-1)
    rows_loop(h, hcut, lambda r, m: sm.__setitem__((pl.ds(r, m), slice(None)), behind[pl.ds(r, m), :].astype(dtype)))
    send(3, sm.at[pl.ds(0, h)], rm.at[pl.ds(0, h)], minus)
    links.arrived(slots[0], ra, plus)
    rows_loop(
        h,
        hcut,
        lambda r, m: sp.__setitem__(
            (pl.ds(r, m), slice(None)),
            (ahead[pl.ds(r, m), :] + ra[pl.ds(r, m), :].astype(F32)).astype(dtype),
        ),
    )
    send(4, sp.at[pl.ds(0, h)], rp.at[pl.ds(0, h)], plus)
    links.arrived(slots[1], rb, plus)
    rows_loop(
        h,
        hcut,
        lambda r, m: sm.__setitem__(
            (pl.ds(h + r, m), slice(None)),
            (behind[pl.ds(h + r, m), :] + rb[pl.ds(r, m), :].astype(F32)).astype(dtype),
        ),
    )
    send(5, sm.at[pl.ds(h, h)], rm.at[pl.ds(h, h)], minus)
    own = slab(0)
    links.arrived(slots[2], rp.at[pl.ds(h, h)], plus)
    links.arrived(slots[3], rm.at[pl.ds(0, h)], plus)
    links.arrived(slots[4], rp.at[pl.ds(0, h)], plus)
    links.arrived(slots[5], rm.at[pl.ds(h, h)], plus)
    rows_loop(
        n,
        cut,
        lambda r, m: out.__setitem__(
            (pl.ds(r, m), slice(None)),
            own[pl.ds(r, m), :] + (rp[pl.ds(r, m), :].astype(F32) + rm[pl.ds(r, m), :].astype(F32)),
        ),
    )
    for copy in sent:
        copy.wait_send()


def stage_bufs(n, dtype):
    h = n // 2
    shapes = [(n, K), (n, K), (n, K), (h, K), (h, K), (n, K), (n, K)]
    return [pltpu.VMEM(shape, dtype) for shape in shapes]


STEP_SCRATCH = [
    pltpu.VMEM((2048, 1024), BF16),
    pltpu.VMEM((4, 512, K), F32),
    pltpu.VMEM((512, K), F32),
    pltpu.VMEM((128, K), F32),
    pltpu.VMEM((32, K), F32),
    pltpu.VMEM((512, 1024), F32),
    pltpu.VMEM((512, 1024), F32),
    pltpu.VMEM((1024, K), F32),
    pltpu.VMEM((1024, K), F32),
    *stage_bufs(512, BF16),
    *stage_bufs(128, F32),
    *stage_bufs(32, F32),
]


def power_step(links, place, xf, xt, proj, z_ref, g_ref, y_ref, scratch):
    yb, img, t1, t2, t3, za, ga, mine, theirs = scratch[:9]
    bufs = [scratch[9 + 7 * i : 16 + 7 * i] for i in range(3)]
    u, v, w = (place.coord[a] for a in "uvw")

    def image_slab(d):
        dst = img.at[d % 4]
        start = ((u + d + 4) % 4) * 512

        def part(r, m):
            dst[pl.ds(r, m), :] = jnp.dot(
                xt[pl.ds(mo(start + r, 128), m), :], proj[...], preferred_element_type=F32
            )

        rows_loop(512, 128, part)
        return dst

    scatter_stage(links, place, "u", image_slab, 512, BF16, bufs[0], t1)
    scatter_stage(
        links, place, "v", lambda d: t1.at[pl.ds(mo(((v + d + 4) % 4) * 128, 128), 128)], 128, F32, bufs[1], t2
    )
    scatter_stage(
        links, place, "w", lambda d: t2.at[pl.ds(mo(((w + d + 4) % 4) * 32, 32), 32)], 32, F32, bufs[2], t3
    )
    image = t3[...] * (1.0 / ROWS)
    high = image.astype(BF16)
    y_ref[:, 0:K] = high
    y_ref[:, K : 2 * K] = (image - high.astype(F32)).astype(BF16)
    own = mo((u * 16 + v * 4 + w) * 32, 32)
    yb[pl.ds(own, 32), :] = y_ref[...]
    for axis, base, n in (("w", (u * 16 + v * 4) * 32, 32), ("v", u * 512, 128)):
        stage = GatherStage(links, place, axis, yb, base, n, source=y_ref if axis == "w" else None)
        stage.start()
        stage.relay()
        stage.finish()

    def consume(d, first=False):
        start = ((u + d + 4) % 4) * 512
        rows = pl.ds(mo(start, 512), 512)

        def product(r, m):
            term = jnp.dot(xf[pl.ds(r, m), pl.ds(mo(start, 512), 512)], yb[rows, :], preferred_element_type=F32)
            za[pl.ds(r, m), :] = term if first else za[pl.ds(r, m), :] + term

        rows_loop(512, 128, product)

        def gram(r, m):
            term = lax.dot_general(
                yb[rows, pl.ds(r, m)], yb[rows, :], (((0,), (0,)), ((), ())), preferred_element_type=F32
            )
            ga[pl.ds(r, m), :] = term if first else ga[pl.ds(r, m), :] + term

        rows_loop(512, 128, gram)

    last = GatherStage(links, place, "u", yb, 0, 512)
    last.start()
    consume(0, first=True)
    last.relay()
    consume(1)
    consume(-1)
    last.finish()
    consume(2)
    mine[0:512, :] = za[:, 0:K] + za[:, K : 2 * K]
    cross = ga[:, K : 2 * K]
    mine[512:1024, :] = ga[:, 0:K] + (cross + cross.T)
    swap = links.copy(links.slot(), mine, theirs, place.partner())
    swap.start()
    swap.wait()
    z_ref[...] = mine[0:512, :] + theirs[0:512, :]
    g_ref[...] = mine[512:1024, :] + theirs[512:1024, :]


FIRST_SLOTS = 80


def first_kernel(
    e_ref, sb_ref, s0_ref, s1_ref, lab_ref,
    xf, xt, z_ref, g_ref, y_ref, labs_ref,
    send, recv, packed, xr, b0, sums, pa, pb, proj, *scratch,
):
    links, place = Links(send, recv), Place()
    u, v, w, k = (*(place.coord[a] for a in "uvw"), place.k)
    partner = place.partner()
    greet([place.along(a, d) for a in "uvw" for d in (1, -1, 2)] + [partner])
    own = mo((u * 16 + v * 4 + w) * 32, 32)
    g1 = GatherStage(links, place, "w", b0, (u * 16 + v * 4) * 32, 32, source=sb_ref)
    g1.start()
    b0[pl.ds(own, 32), :] = sb_ref[...]
    swap_labels = links.copy(links.slot(), lab_ref, labs_ref.at[pl.ds(mo(k * 256, 256), 256)], partner)
    swap_labels.start()
    labs_ref[pl.ds(mo(k * 256, 256), 256), :] = lab_ref[...]

    def pack(t, carry):
        x, y = t // 4, t % 4
        src = mo(((x // 2) * 4 + y) * 512, 512)
        packed[0, :, pl.ds(mo(t * 128, 128), 128)] = jnp.dot(
            e_ref[:, pl.ds(src, 512)], s0_ref[x % 2], preferred_element_type=F32
        ).astype(BF16)
        near = jnp.dot(e_ref[:, pl.ds(mo(t * 128, 128), 128)], s1_ref[0], preferred_element_type=F32)
        far = jnp.dot(e_ref[:, pl.ds(mo(2048 + t * 128, 128), 128)], s1_ref[1], preferred_element_type=F32)
        packed[1, :, pl.ds(mo(t * 128, 128), 128)] = (near + far).astype(BF16)
        return carry

    lax.fori_loop(0, 16, pack, 0)
    swap_rows = links.copy(links.slot(), packed.at[1 - k], xr.at[pl.ds(mo(k * 256, 256), 256)], partner)
    swap_rows.start()
    xr[pl.ds(mo(k * 256, 256), 256), :] = packed[k]
    g1.relay()
    g1.finish()
    g2 = GatherStage(links, place, "v", b0, u * 512, 128)
    g2.start()
    swap_rows.wait()

    def exchange(stage, axis, value):
        here = place.coord[axis]
        sums[stage, here] = value
        copies = []
        for d in (1, -1, 2):
            copy = links.copy(links.slot(), sums.at[stage, here], sums.at[stage, here], place.along(axis, d))
            copy.start()
            copies.append((copy, d))

        def done():
            for copy, _ in copies:
                copy.wait()
            return (sums[stage, 0] + sums[stage, 1]) + (sums[stage, 2] + sums[stage, 3])

        return done

    ones = jnp.ones((8, 512), BF16)
    done = exchange(0, "u", jnp.dot(ones, xr[...], preferred_element_type=F32))
    g2.relay()
    done = exchange(1, "v", done())
    g2.finish()
    g3 = GatherStage(links, place, "u", b0, 0, 512)
    g3.start()
    done = exchange(2, "w", done())
    average = done()[0:1, :] / ROWS
    g3.relay()

    def center(r, m):
        xf[pl.ds(r, m), :] = (xr[pl.ds(r, m), :].astype(F32) - average).astype(BF16)

    rows_loop(512, 32, center)

    def turn(t, carry):
        lanes = pl.ds(mo(t * 128, 128), 128)
        xt[lanes, :] = xf[:, lanes].T
        return carry

    lax.fori_loop(0, 16, turn, 0)
    g3.finish()

    def product(r, m):
        pa[pl.ds(r, m), :] = jnp.dot(xf[pl.ds(r, m), :], b0[...], preferred_element_type=F32)

    rows_loop(512, 128, product)
    swap = links.copy(links.slot(), pa, pb, partner)
    swap.start()
    swap_labels.wait()
    swap.wait()

    def total(r, m):
        proj[pl.ds(r, m), :] = (pa[pl.ds(r, m), :] + pb[pl.ds(r, m), :]).astype(BF16)

    rows_loop(512, 128, total)
    power_step(links, place, xf, xt, proj, z_ref, g_ref, y_ref, scratch)


def next_kernel(xf, xt, proj, z_ref, g_ref, y_ref, send, recv, *scratch):
    links, place = Links(send, recv), Place()
    greet([place.along(a, d) for a in "uvw" for d in (1, -1)] + [place.partner()])
    power_step(links, place, xf, xt, proj, z_ref, g_ref, y_ref, scratch)


def nearest_kernel(units, own_labels, labs, limit, out, send, recv, ub, best, theirs):
    links, place = Links(send, recv), Place()
    z, k, xl = place.z, place.k, place.x % 2
    flip = 1 - 2 * xl
    across = place.at(flip, 0, 0, k)
    up, down = place.at(0, 0, 1, k), place.at(0, 0, -1, k)
    partner = place.partner()
    greet([across, up, down, partner])
    own = ub.at[z, xl]
    own[0:256, :] = units[pl.ds(mo(k * 256, 256), 256), :]
    own[256:272, :] = own_labels[...]
    slots = [links.slot() for _ in range(8)]

    def zed(d):
        return (z + d + 4) % 4

    def send_all(pairs):
        copies = [links.copy(slots[i], ref, ref, device) for i, ref, device in pairs]
        for copy in copies:
            copy.start()
        return copies

    def got(i, ref):
        links.arrived(slots[i], ref, partner)

    @pl.when(k == 0)
    def _():
        sent = send_all([(0, own, across)])
        got(0, ub.at[z, 1 - xl])
        sent += send_all([(1, ub.at[z], up), (2, ub.at[z], down)])
        got(1, ub.at[zed(-1)])
        sent += send_all([(3, ub.at[zed(-1), 0], up)])
        got(2, ub.at[zed(1)])
        sent += send_all([(4, ub.at[zed(1), 1], down)])
        got(3, ub.at[zed(2), 0])
        got(4, ub.at[zed(2), 1])
        for copy in sent:
            copy.wait_send()

    @pl.when(k == 1)
    def _():
        sent = send_all([(0, own, across), (1, own, up), (2, own, down)])
        got(1, ub.at[zed(-1), xl])
        low = ub.at[zed(-1), xl, pl.ds(0, 144)]
        sent += send_all([(3, low, up), (5, ub.at[zed(-1), xl], across)])
        got(2, ub.at[zed(1), xl])
        high = ub.at[zed(1), xl, pl.ds(144, 128)]
        sent += send_all([(4, high, down), (6, ub.at[zed(1), xl], across)])
        got(3, ub.at[zed(2), xl, pl.ds(0, 144)])
        got(4, ub.at[zed(2), xl, pl.ds(144, 128)])
        sent += send_all([(7, ub.at[zed(2), xl], across)])
        got(0, ub.at[z, 1 - xl])
        got(5, ub.at[zed(-1), 1 - xl])
        got(6, ub.at[zed(1), 1 - xl])
        got(7, ub.at[zed(2), 1 - xl])
        for copy in sent:
            copy.wait_send()

    best[...] = jnp.full((512, 128), -1.0, F32)
    bound = limit[0:1, :]
    lane = lax.broadcasted_iota(jnp.int32, (1, 128), 1)
    mine_first = (z * 4 + xl * 2) * 256

    def block(b, carry):
        zz, xx = b // 2, b % 2
        labels = ub[zz, xx, 256:272, :][0:1, :].astype(F32)
        first = (zz * 4 + xx * 2 + k) * 256

        def part(r, m):
            score = lax.dot_general(
                units[pl.ds(r, m), :], ub[zz, xx, 0:256, :], (((1,), (1,)), ((), ())), preferred_element_type=F32
            )
            rows = lax.broadcasted_iota(jnp.int32, (m, 128), 0) + (mine_first + r)
            label = labs[pl.ds(r, m), :].astype(F32)
            top = best[pl.ds(r, m), :]
            for t in range(2):
                other = lane + (first + t * 128)
                use = (label == labels[:, t * 128 : t * 128 + 128]) & (other < bound) & (other != rows)
                top = jnp.maximum(top, jnp.where(use, score[:, t * 128 : t * 128 + 128], -1.0))
            best[pl.ds(r, m), :] = top

        rows_loop(512, 128, part)
        return carry

    lax.fori_loop(0, 8, block, 0)
    best[...] = jnp.broadcast_to(jnp.max(best[...], axis=1, keepdims=True), (512, 128))
    swap = links.copy(
        links.slot(), best.at[pl.ds(mo((1 - k) * 256, 256), 256)], theirs, partner
    )
    swap.start()
    swap.wait()
    out[...] = jnp.maximum(best[pl.ds(mo(k * 256, 256), 256), :], theirs[...])


def comm_call(kernel, outs, scratch, cid, slots, name):
    vmem = pl.BlockSpec(memory_space=pltpu.VMEM)

    def call(*args):
        return pl.pallas_call(
            kernel,
            out_shape=outs,
            in_specs=[vmem] * len(args),
            out_specs=jax.tree.map(lambda _: vmem, outs),
            scratch_shapes=[pltpu.SemaphoreType.DMA((slots,)), pltpu.SemaphoreType.DMA((slots,)), *scratch],
            compiler_params=pltpu.CompilerParams(
                collective_id=cid, has_side_effects=True, vmem_limit_bytes=VMEM_LIMIT
            ),
            name=name,
        )(*args)

    return call


def selections():
    s0 = np.zeros((2, 512, 128), np.float32)
    s1 = np.zeros((2, 128, 128), np.float32)
    r = np.arange(32)
    for lo in range(2):
        for z in range(4):
            s0[lo, z * 128 + lo * 64 + r, z * 32 + r] = 1
        for hi in range(2):
            s1[hi, (lo * 2 + 1) * 32 + r, (hi * 2 + lo) * 32 + r] = 1
    return jnp.asarray(s0, BF16), jnp.asarray(s1, BF16)


def sub(x, c):
    return jnp.broadcast_to(x[c : c + 1, :], (8, 128))


def lane(x, j):
    return jnp.broadcast_to(x[:, j : j + 1], (8, 128))


HIGH = lax.Precision.HIGHEST
TT = (((1,), (1,)), ((), ()))


def dot6(a, b):
    return lax.dot_general(a, b, TT, precision=HIGH, preferred_element_type=F32)


def split(a):
    high = a.astype(BF16)
    return high, (a - high.astype(F32)).astype(BF16)


def dot3(a, b):
    def one(p, q):
        return lax.dot_general(p, q, TT, preferred_element_type=F32)

    return one(a[0], b[0]) + (one(a[0], b[1]) + one(a[1], b[0]))


def inverse_factor_128(a_rows, w_rows, between):
    row_id = lax.broadcasted_iota(jnp.int32, (8, 128), 0)
    out = []
    for p in range(16):
        j0 = 8 * p
        va, vw = a_rows[p], w_rows[p]
        diag = [lane(va, j0 + b) for b in range(8)]
        tops, inverses, pivots, rows = [], [], [], []
        for c in range(8):
            pivot = sub(diag[c], c)
            q = 1.0 / pivot
            f = jnp.where(row_id > c, diag[c] * q, 0.0)
            ua, uw = sub(va, c), sub(vw, c)
            row = {b: sub(diag[b], c) for b in range(c + 1, 8)}
            va, vw = va - f * ua, vw - f * uw
            for b in range(c + 1, 8):
                diag[b] = diag[b] - f * row[b]
            tops.append((ua, uw))
            inverses.append(q)
            pivots.append(pivot)
            rows.append(row)
        scale = pivots[0]
        for c in range(1, 8):
            scale = jnp.where(row_id == c, pivots[c], scale)
        out.append(vw * lax.rsqrt(scale))
        for i in range(p + 1, 16):
            below = [lane(a_rows[i], j0 + b) for b in range(8)]
            a, w = a_rows[i], w_rows[i]
            for c in range(8):
                f = below[c] * inverses[c]
                a, w = a - f * tops[c][0], w - f * tops[c][1]
                for b in range(c + 1, 8):
                    below[b] = below[b] - f * rows[c][b]
            a_rows[i], w_rows[i] = a, w
        between(p)
    return out


def factor_apply(s, zs, chunks, out, ad, wp, lp):
    row_id = lax.broadcasted_iota(jnp.int32, (8, 128), 0)
    lane_id = lax.broadcasted_iota(jnp.int32, (8, 128), 1)
    ad[...] = s[0:128, 0:128]
    wp[...] = jnp.zeros((128, 128), F32)
    lp[...] = jnp.zeros((512, 128), F32)

    def step(kb, carry):
        prev = pl.ds(mo(jnp.maximum(kb - 1, 0) * 128, 128), 128)
        col = pl.ds(mo(kb * 128, 128), 128)
        a_rows = [ad[8 * i : 8 * i + 8, :] for i in range(16)]
        w_rows = [jnp.where(lane_id == row_id + 8 * i, 1.0, 0.0) for i in range(16)]
        inverse = split(wp[...])

        def gram_chunk(i):
            r = slice(i * 128, i * 128 + 128)
            s[r, :] = s[r, :] - dot6(lp[r, :], lp[...])

        def row_chunk(lo, n):
            r = slice(lo, lo + n)
            c = dot3(split(zs[r, prev]), inverse)
            out[r, prev] = c
            zs[r, :] = zs[r, :] - dot3(split(c), split(lp[...]))

        work = [functools.partial(gram_chunk, i) for i in range(4)]
        work += [functools.partial(row_chunk, lo, n) for lo, n in chunks]

        def between(p):
            if p % 2 == 1 and work:
                work.pop(0)()
            while p == 15 and work:
                work.pop(0)()

        rows = inverse_factor_128(a_rows, w_rows, between)
        for i in range(16):
            wp[8 * i : 8 * i + 8, :] = rows[i]
        new = dot6(s[:, col], wp[...])
        below = lax.broadcasted_iota(jnp.int32, (512, 128), 0) >= (kb + 1) * 128
        lp[...] = jnp.where(below, new, 0.0)
        following = pl.ds(mo(jnp.minimum(kb + 1, 3) * 128, 128), 128)
        ad[...] = s[following, following] - dot6(lp[following, :], lp[following, :])
        return carry

    lax.fori_loop(0, 4, step, 0)
    inverse = split(wp[...])
    for lo, n in chunks:
        out[lo : lo + n, 384:512] = dot3(split(zs[lo : lo + n, 384:512]), inverse)


CHUNKS = [(i * 128, 128) for i in range(4)]
FACTOR_SCRATCH = [
    pltpu.VMEM((512, 512), F32),
    pltpu.VMEM((544, 512), F32),
    pltpu.VMEM((544, 512), F32),
    pltpu.VMEM((128, 128), F32),
    pltpu.VMEM((128, 128), F32),
    pltpu.VMEM((512, 128), F32),
]


def middle_kernel(g_ref, z_ref, proj, s, zs, out, ad, wp, lp):
    s[...] = g_ref[...]
    zs[0:512, :] = z_ref[...]
    factor_apply(s, zs, CHUNKS, out, ad, wp, lp)
    proj[...] = out[0:512, :].astype(BF16)


def last_kernel(g_ref, z_ref, y_ref, unit, subspace, s, zs, out, ad, wp, lp):
    s[...] = g_ref[...]
    zs[0:512, :] = z_ref[...]
    zs[512:544, :] = y_ref[:, 0:K].astype(F32) + y_ref[:, K : 2 * K].astype(F32)
    factor_apply(s, zs, CHUNKS + [(512, 32)], out, ad, wp, lp)
    for i in range(4):
        coords = out[i * 128 : i * 128 + 128, :]
        size = jnp.sum(coords * coords, axis=1, keepdims=True) + EPS
        unit[i * 128 : i * 128 + 128, :] = (coords * lax.rsqrt(size)).astype(BF16)
    subspace[...] = out[512:544, :] * math.sqrt(D)


def local_call(kernel, outs, name):
    vmem = pl.BlockSpec(memory_space=pltpu.VMEM)

    def call(*args):
        return pl.pallas_call(
            kernel,
            out_shape=outs,
            in_specs=[vmem] * len(args),
            out_specs=jax.tree.map(lambda _: vmem, outs),
            scratch_shapes=FACTOR_SCRATCH,
            compiler_params=pltpu.CompilerParams(vmem_limit_bytes=VMEM_LIMIT),
            name=name,
        )(*args)

    return call


def body(embeddings, start_basis, cluster_ids, valid_counts):
    step_out = [
        jax.ShapeDtypeStruct((512, K), F32),
        jax.ShapeDtypeStruct((K, K), F32),
        jax.ShapeDtypeStruct((32, 2 * K), BF16),
    ]
    x_out = [jax.ShapeDtypeStruct((512, 2048), BF16), jax.ShapeDtypeStruct((2048, 512), BF16)]
    labels = cluster_ids.astype(BF16)
    label_columns = jnp.broadcast_to(labels[:, None], (256, 128))
    s0, s1 = selections()
    xf, xt, z, gram, image, labs = comm_call(
        first_kernel,
        [*x_out, *step_out, jax.ShapeDtypeStruct((512, 128), BF16)],
        [
            pltpu.VMEM((2, 256, 2048), BF16),
            pltpu.VMEM((512, 2048), BF16),
            pltpu.VMEM((2048, K), BF16),
            pltpu.VMEM((3, 4, 8, 2048), F32),
            pltpu.VMEM((512, K), F32),
            pltpu.VMEM((512, K), F32),
            pltpu.VMEM((512, K), BF16),
            *STEP_SCRATCH,
        ],
        0,
        FIRST_SLOTS,
        "first_step",
    )(embeddings, start_basis, s0, s1, label_columns)

    proj = local_call(middle_kernel, jax.ShapeDtypeStruct((512, K), BF16), "middle_factor")(gram, z)
    z, gram, image = comm_call(next_kernel, step_out, STEP_SCRATCH, 1, FIRST_SLOTS, "next_step")(xf, xt, proj)
    unit, subspace = local_call(
        last_kernel,
        [jax.ShapeDtypeStruct((512, K), BF16), jax.ShapeDtypeStruct((32, K), F32)],
        "last_factor",
    )(gram, z, image)
    limit = jnp.broadcast_to(valid_counts[None, :], (8, 128))
    own_labels = jnp.broadcast_to(jnp.concatenate([labels, labels])[None, :], (16, 512))
    nearest = comm_call(
        nearest_kernel,
        jax.ShapeDtypeStruct((256, 128), F32),
        [
            pltpu.VMEM((4, 2, 272, K), BF16),
            pltpu.VMEM((512, 128), F32),
            pltpu.VMEM((256, 128), F32),
        ],
        2,
        16,
        "nearest",
    )(unit, own_labels, labs, limit)
    return (subspace, nearest[:, 0])


def solution(mesh):
    placed = (
        P(("cluster", "member"), None),
        P(("cluster", "member"), None),
        P(("cluster", "member")),
        P("cluster"),
    )
    return jax.shard_map(
        body,
        mesh=mesh,
        in_specs=placed,
        out_specs=(P(("cluster", "member"), None), P(("cluster", "member"))),
        check_vma=False,
    )
```

```python
import functools
import math

import jax
import jax.numpy as jnp
import numpy as np
from jax import lax
from jax.experimental import pallas as pl
from jax.experimental.pallas import tpu as pltpu
from jax.sharding import PartitionSpec as P

EPS = 1e-06
MESH = pl.DeviceIdType.MESH
F32 = jnp.float32
BF16 = jnp.bfloat16
D = 4096
K = 512
ROWS = 32768
VMEM_LIMIT = 60 * 1024 * 1024


class Links:
    def __init__(self, send, recv):
        self.send, self.recv, self.used = send, recv, 0

    def slot(self):
        self.used += 1
        return self.used - 1

    def copy(self, slot, src, dst, device):
        return pltpu.make_async_remote_copy(
            src_ref=src,
            dst_ref=dst,
            send_sem=self.send.at[slot],
            recv_sem=self.recv.at[slot],
            device_id=device,
            device_id_type=MESH,
        )

    def arrived(self, slot, dst, device):
        self.copy(slot, dst, dst, device).wait_recv()


class Place:
    def __init__(self):
        c, m = lax.axis_index("cluster"), lax.axis_index("member")
        self.x = (c // 4) * 2 + (m // 2) % 2
        self.y = c % 4
        self.z = m // 4
        self.k = m % 2
        k, o = self.k, 1 - self.k
        self.coord = {
            "u": self.x * o + self.y * k,
            "v": self.z,
            "w": self.y * o + self.x * k,
        }

    def at(self, dx, dy, dz, core):
        x = (self.x + dx + 4) % 4
        y = (self.y + dy + 4) % 4
        z = (self.z + dz + 4) % 4
        return ((x // 2) * 4 + y, z * 4 + (x % 2) * 2 + core)

    def along(self, axis, d):
        k, o = self.k, 1 - self.k
        if axis == "u":
            return self.at(d * o, d * k, 0, k)
        if axis == "v":
            return self.at(0, 0, d, k)
        return self.at(d * k, d * o, 0, k)

    def partner(self):
        return self.at(0, 0, 0, 1 - self.k)


def greet(devices):
    barrier = pltpu.get_barrier_semaphore()
    for device in devices:
        pl.semaphore_signal(barrier, inc=1, device_id=device, device_id_type=MESH)
    pl.semaphore_wait(barrier, len(devices))


def mo(i, n):
    return pl.multiple_of(i, n)


class GatherStage:
    def __init__(self, links, place, axis, buf, base, n, stride, source=None):
        self.links, self.buf, self.n, self.h = links, buf, n, n // 2
        self.base, self.stride, self.coord = base, stride, place.coord[axis]
        self.plus, self.minus = place.along(axis, 1), place.along(axis, -1)
        self.slots = [links.slot() for _ in range(4)]
        self.source = source
        self.sent = []

    def region(self, d, part=None):
        start = mo(self.base + ((self.coord + d + 4) % 4) * self.stride, self.n)
        if part is None:
            return self.buf.at[pl.ds(start, self.n)]
        return self.buf.at[pl.ds(mo(start + part * self.h, self.h), self.h)]

    def _send(self, i, src, dst, device):
        copy = self.links.copy(self.slots[i], src, dst, device)
        copy.start()
        self.sent.append(copy)

    def start(self):
        own = self.region(0)
        src = own if self.source is None else self.source
        self._send(0, src, own, self.plus)
        self._send(1, src, own, self.minus)

    def relay(self):
        self.links.arrived(self.slots[0], self.region(-1), self.plus)
        first = self.region(-1, 0)
        self._send(2, first, first, self.plus)
        self.links.arrived(self.slots[1], self.region(1), self.plus)
        second = self.region(1, 1)
        self._send(3, second, second, self.minus)

    def far(self):
        self.links.arrived(self.slots[2], self.region(2, 0), self.plus)
        self.links.arrived(self.slots[3], self.region(2, 1), self.plus)

    def drain(self):
        for copy in self.sent:
            copy.wait_send()


class DirectStage(GatherStage):
    def __init__(self, links, place, axis, *rest, **more):
        super().__init__(links, place, axis, *rest, **more)
        self.opposite = place.along(axis, 2)

    def start(self):
        super().start()
        own = self.region(0)
        src = own if self.source is None else self.source
        self._send(2, src, own, self.opposite)

    def near(self):
        self.links.arrived(self.slots[0], self.region(-1), self.plus)
        self.links.arrived(self.slots[1], self.region(1), self.plus)

    def far(self):
        self.links.arrived(self.slots[2], self.region(2), self.plus)


def flood(links, place, buf, source):
    u, v, w = (place.coord[a] for a in "uvw")

    def ahead(c, d):
        return (c + d + 4) % 4

    own = {0: source}
    wst = DirectStage(links, place, "w", buf, (u * 16 + v * 4) * 32, 32, 32, source=source)
    vst = {
        e: GatherStage(links, place, "v", buf, u * 512 + ahead(w, e) * 32, 32, 128, source=own.get(e))
        for e in (0, -1, 1, 2)
    }
    ust = {
        e: GatherStage(links, place, "u", buf, v * 128 + ahead(w, e) * 32, 32, 512, source=own.get(e))
        for e in (0, -1, 1, 2)
    }
    big = {f: GatherStage(links, place, "u", buf, ahead(v, f) * 128, 128, 512) for f in (-1, 1, 2)}
    wst.start()
    vst[0].start()
    ust[0].start()
    yield None
    wst.near()
    for e in (-1, 1):
        vst[e].start()
        ust[e].start()
    vst[0].relay()
    ust[0].relay()
    yield None
    wst.far()
    vst[2].start()
    ust[2].start()
    for e in (-1, 1):
        vst[e].relay()
        ust[e].relay()
    yield None
    vst[2].relay()
    big[-1].start()
    big[1].start()
    ust[2].relay()
    for e in (0, -1, 1, 2):
        vst[e].far()
    big[2].start()
    yield (0,)
    for f in (-1, 1, 2):
        big[f].relay()
    yield (1, -1)
    for e in (0, -1, 1, 2):
        ust[e].far()
    for f in (-1, 1, 2):
        big[f].far()
    yield (2,)
    for stage in [wst, *vst.values(), *ust.values(), *big.values()]:
        stage.drain()


def rows_loop(total, step, fn):
    if total <= step:
        fn(0, total)
        return

    def body(i, carry):
        fn(mo(i * step, step), step)
        return carry

    lax.fori_loop(0, total // step, body, 0)


def scatter_stage(links, place, axis, slab, n, dtype, bufs, out):
    h = n // 2
    s2, sp, sm, ra, rb, rp, rm = bufs
    plus, minus = place.along(axis, 1), place.along(axis, -1)
    slots = [links.slot() for _ in range(6)]
    sent = []
    cut = min(n, 128)
    hcut = min(h, 128)

    def send(i, src, dst, device):
        copy = links.copy(slots[i], src, dst, device)
        copy.start()
        sent.append(copy)

    term = slab(2)
    rows_loop(n, cut, lambda r, m: s2.__setitem__((pl.ds(r, m), slice(None)), term[pl.ds(r, m), :].astype(dtype)))
    send(0, s2.at[pl.ds(0, h)], ra, plus)
    send(1, s2.at[pl.ds(h, h)], rb, minus)
    ahead = slab(1)
    rows_loop(h, hcut, lambda r, m: sp.__setitem__((pl.ds(h + r, m), slice(None)), ahead[pl.ds(h + r, m), :].astype(dtype)))
    send(2, sp.at[pl.ds(h, h)], rp.at[pl.ds(h, h)], plus)
    behind = slab(-1)
    rows_loop(h, hcut, lambda r, m: sm.__setitem__((pl.ds(r, m), slice(None)), behind[pl.ds(r, m), :].astype(dtype)))
    send(3, sm.at[pl.ds(0, h)], rm.at[pl.ds(0, h)], minus)
    links.arrived(slots[0], ra, plus)
    rows_loop(
        h,
        hcut,
        lambda r, m: sp.__setitem__(
            (pl.ds(r, m), slice(None)),
            (ahead[pl.ds(r, m), :] + ra[pl.ds(r, m), :].astype(F32)).astype(dtype),
        ),
    )
    send(4, sp.at[pl.ds(0, h)], rp.at[pl.ds(0, h)], plus)
    links.arrived(slots[1], rb, plus)
    rows_loop(
        h,
        hcut,
        lambda r, m: sm.__setitem__(
            (pl.ds(h + r, m), slice(None)),
            (behind[pl.ds(h + r, m), :] + rb[pl.ds(r, m), :].astype(F32)).astype(dtype),
        ),
    )
    send(5, sm.at[pl.ds(h, h)], rm.at[pl.ds(h, h)], minus)
    own = slab(0)
    links.arrived(slots[2], rp.at[pl.ds(h, h)], plus)
    links.arrived(slots[3], rm.at[pl.ds(0, h)], plus)
    links.arrived(slots[4], rp.at[pl.ds(0, h)], plus)
    links.arrived(slots[5], rm.at[pl.ds(h, h)], plus)
    rows_loop(
        n,
        cut,
        lambda r, m: out.__setitem__(
            (pl.ds(r, m), slice(None)),
            own[pl.ds(r, m), :] + (rp[pl.ds(r, m), :].astype(F32) + rm[pl.ds(r, m), :].astype(F32)),
        ),
    )
    for copy in sent:
        copy.wait_send()


def sub(x, c):
    return jnp.broadcast_to(x[c : c + 1, :], (8, 128))


def lane(x, j):
    return jnp.broadcast_to(x[:, j : j + 1], (8, 128))


HIGH = lax.Precision.HIGHEST
TT = (((1,), (1,)), ((), ()))


def dot6(a, b):
    return lax.dot_general(a, b, TT, precision=HIGH, preferred_element_type=F32)


def split(a):
    high = a.astype(BF16)
    return high, (a - high.astype(F32)).astype(BF16)


def dot3(a, b):
    def one(p, q):
        return lax.dot_general(p, q, TT, preferred_element_type=F32)

    return one(a[0], b[0]) + (one(a[0], b[1]) + one(a[1], b[0]))


def inverse_factor_128(a_rows, w_rows, between):
    row_id = lax.broadcasted_iota(jnp.int32, (8, 128), 0)
    out = []
    for p in range(16):
        j0 = 8 * p
        va, vw = a_rows[p], w_rows[p]
        diag = [lane(va, j0 + b) for b in range(8)]
        tops, inverses, pivots, rows = [], [], [], []
        for c in range(8):
            pivot = sub(diag[c], c)
            q = 1.0 / pivot
            f = jnp.where(row_id > c, diag[c] * q, 0.0)
            ua, uw = sub(va, c), sub(vw, c)
            row = {b: sub(diag[b], c) for b in range(c + 1, 8)}
            va, vw = va - f * ua, vw - f * uw
            for b in range(c + 1, 8):
                diag[b] = diag[b] - f * row[b]
            tops.append((ua, uw))
            inverses.append(q)
            pivots.append(pivot)
            rows.append(row)
        scale = pivots[0]
        for c in range(1, 8):
            scale = jnp.where(row_id == c, pivots[c], scale)
        out.append(vw * lax.rsqrt(scale))
        for i in range(p + 1, 16):
            below = [lane(a_rows[i], j0 + b) for b in range(8)]
            a, w = a_rows[i], w_rows[i]
            for c in range(8):
                f = below[c] * inverses[c]
                a, w = a - f * tops[c][0], w - f * tops[c][1]
                for b in range(c + 1, 8):
                    below[b] = below[b] - f * rows[c][b]
            a_rows[i], w_rows[i] = a, w
        between(p)
    return out


def factor_apply(s, zs, chunks, out, ad, wp, lp):
    row_id = lax.broadcasted_iota(jnp.int32, (8, 128), 0)
    lane_id = lax.broadcasted_iota(jnp.int32, (8, 128), 1)
    ad[...] = s[0:128, 0:128]
    wp[...] = jnp.zeros((128, 128), F32)
    lp[...] = jnp.zeros((512, 128), F32)

    def step(kb, carry):
        prev = pl.ds(mo(jnp.maximum(kb - 1, 0) * 128, 128), 128)
        col = pl.ds(mo(kb * 128, 128), 128)
        a_rows = [ad[8 * i : 8 * i + 8, :] for i in range(16)]
        w_rows = [jnp.where(lane_id == row_id + 8 * i, 1.0, 0.0) for i in range(16)]
        inverse = split(wp[...])

        def gram_chunk(i):
            r = slice(i * 128, i * 128 + 128)
            s[r, :] = s[r, :] - dot6(lp[r, :], lp[...])

        def row_chunk(lo, n):
            r = slice(lo, lo + n)
            c = dot3(split(zs[r, prev]), inverse)
            out[r, prev] = c
            zs[r, :] = zs[r, :] - dot3(split(c), split(lp[...]))

        work = [functools.partial(gram_chunk, i) for i in range(4)]
        work += [functools.partial(row_chunk, lo, n) for lo, n in chunks]

        def between(p):
            if p % 2 == 1 and work:
                work.pop(0)()
            while p == 15 and work:
                work.pop(0)()

        rows = inverse_factor_128(a_rows, w_rows, between)
        for i in range(16):
            wp[8 * i : 8 * i + 8, :] = rows[i]
        new = dot6(s[:, col], wp[...])
        below = lax.broadcasted_iota(jnp.int32, (512, 128), 0) >= (kb + 1) * 128
        lp[...] = jnp.where(below, new, 0.0)
        following = pl.ds(mo(jnp.minimum(kb + 1, 3) * 128, 128), 128)
        ad[...] = s[following, following] - dot6(lp[following, :], lp[following, :])
        return carry

    lax.fori_loop(0, 4, step, 0)
    inverse = split(wp[...])
    for lo, n in chunks:
        out[lo : lo + n, 384:512] = dot3(split(zs[lo : lo + n, 384:512]), inverse)


def selections():
    s0 = np.zeros((2, 512, 128), np.float32)
    s1 = np.zeros((2, 128, 128), np.float32)
    r = np.arange(32)
    for lo in range(2):
        for y in range(4):
            s0[lo, y * 128 + lo * 64 + r, y * 32 + r] = 1
        for hi in range(2):
            s1[hi, (lo * 2 + 1) * 32 + r, (hi * 2 + lo) * 32 + r] = 1
    return jnp.asarray(s0, BF16), jnp.asarray(s1, BF16)


def bands(n, dtype):
    h = n // 2
    shapes = [(n, K), (n, K), (n, K), (h, K), (h, K), (n, K), (n, K)]
    return [pltpu.VMEM(shape, dtype) for shape in shapes]


CHUNKS = [(i * 128, 128) for i in range(4)]
SCRATCH = {
    "packed": pltpu.VMEM((2, 256, 2048), BF16),
    "raw": pltpu.VMEM((512, 2048), BF16),
    "xf": pltpu.VMEM((512, 2048), BF16),
    "xt": pltpu.VMEM((2048, 512), BF16),
    "b0": pltpu.VMEM((2048, K), BF16),
    "sums": pltpu.VMEM((3, 4, 8, 2048), F32),
    "pa": pltpu.VMEM((512, K), F32),
    "pb": pltpu.VMEM((512, K), F32),
    "proj": pltpu.VMEM((512, K), BF16),
    "y": pltpu.VMEM((2, 32, 2 * K), BF16),
    "yb": pltpu.VMEM((2048, 2 * K), BF16),
    "img": pltpu.VMEM((4, 512, K), F32),
    "t1": pltpu.VMEM((512, K), F32),
    "t2": pltpu.VMEM((128, K), F32),
    "t3": pltpu.VMEM((32, K), F32),
    "za": pltpu.VMEM((512, 2 * K), F32),
    "ga": pltpu.VMEM((512, 2 * K), F32),
    "mine": pltpu.VMEM((1024, K), F32),
    "theirs": pltpu.VMEM((2, 1024, K), F32),
    "bu": bands(512, BF16),
    "bv": bands(128, F32),
    "bw": bands(32, F32),
    "s": pltpu.VMEM((512, 512), F32),
    "zs": pltpu.VMEM((544, 512), F32),
    "out": pltpu.VMEM((544, 512), F32),
    "ad": pltpu.VMEM((128, 128), F32),
    "wp": pltpu.VMEM((128, 128), F32),
    "lp": pltpu.VMEM((512, 128), F32),
    "labs": pltpu.VMEM((512, 128), BF16),
    "lb": pltpu.VMEM((4, 2, 16, 256), BF16),
    "units": pltpu.VMEM((512, K), BF16),
    "ub": pltpu.VMEM((4, 2, 256, K), BF16),
    "best": pltpu.VMEM((512, 128), F32),
    "tops": pltpu.VMEM((2, 8, 512), F32),
}


def first_product(links, place, e_ref, sb_ref, s0_ref, s1_ref, lab_ref, row_ref, m):
    u, v, w, k = (*(place.coord[a] for a in "uvw"), place.k)
    z, xl = place.z, place.x % 2
    partner = place.partner()
    packed, raw, xf, xt, b0, sums = (m[n] for n in ("packed", "raw", "xf", "xt", "b0", "sums"))
    gather = flood(links, place, b0, sb_ref)
    next(gather)
    b0[pl.ds(mo((u * 16 + v * 4 + w) * 32, 32), 32), :] = sb_ref[...]

    def pack(t, carry):
        x, q = t // 4, t % 4
        tiles = [e_ref[:, pl.ds(mo((((x // 2) * 4 + y) * 4 + q) * 128, 128), 128)] for y in range(4)]
        lanes = pl.ds(mo(t * 128, 128), 128)
        packed[0, :, lanes] = jnp.dot(
            jnp.concatenate(tiles, axis=1), s0_ref[x % 2], preferred_element_type=F32
        ).astype(BF16)
        near = jnp.dot(e_ref[:, lanes], s1_ref[0], preferred_element_type=F32)
        far = jnp.dot(e_ref[:, pl.ds(mo(2048 + t * 128, 128), 128)], s1_ref[1], preferred_element_type=F32)
        packed[1, :, lanes] = (near + far).astype(BF16)
        return carry

    lax.fori_loop(0, 16, pack, 0, unroll=4)
    mine = pl.ds(mo(k * 256, 256), 256)
    swap_rows = links.copy(links.slot(), packed.at[1 - k], raw.at[mine], partner)
    swap_rows.start()
    raw[mine, :] = packed[k]
    labs, lb = m["labs"], m["lb"]
    small = [links.copy(links.slot(), lab_ref, labs.at[mine], partner)]
    labs[mine, :] = lab_ref[...]
    lb[z, xl] = row_ref[...]
    for dz in range(4):
        for dx in range(2):
            if dz or dx:
                device = place.at(dx * (1 - 2 * xl), 0, dz, k)
                small.append(links.copy(links.slot(), row_ref, lb.at[z, xl], device))
    for copy in small:
        copy.start()
    next(gather)
    swap_rows.wait()

    def exchange(stage, axis, value):
        here = place.coord[axis]
        sums[stage, here] = value
        copies = []
        for d in (1, -1, 2):
            copy = links.copy(links.slot(), sums.at[stage, here], sums.at[stage, here], place.along(axis, d))
            copy.start()
            copies.append(copy)

        def done():
            for copy in copies:
                copy.wait()
            return (sums[stage, 0] + sums[stage, 1]) + (sums[stage, 2] + sums[stage, 3])

        return done

    done = exchange(0, "u", jnp.dot(jnp.ones((8, 512), BF16), raw[...], preferred_element_type=F32))
    next(gather)
    done = exchange(1, "v", done())
    next(gather)
    done = exchange(2, "w", done())
    average = done()[0:1, :] / ROWS

    def center(r, n):
        xf[pl.ds(r, n), :] = (raw[pl.ds(r, n), :].astype(F32) - average).astype(BF16)

    rows_loop(512, 32, center)

    def turn(t, carry):
        lanes = pl.ds(mo(t * 128, 128), 128)
        xt[lanes, :] = xf[:, lanes].T
        return carry

    lax.fori_loop(0, 16, turn, 0)
    pa, pb, proj = m["pa"], m["pb"], m["proj"]

    def product(d, first=False):
        slab = pl.ds(mo(((u + d + 4) % 4) * 512, 512), 512)
        term = jnp.dot(xf[:, slab], b0[slab, :], preferred_element_type=F32)
        pa[...] = term if first else pa[...] + term

    product(0, first=True)
    next(gather)
    product(1)
    product(-1)
    next(gather)
    product(2)
    next(gather, None)
    swap = links.copy(links.slot(), pa, pb, partner)
    swap.start()
    for copy in small:
        copy.wait()
    swap.wait()
    proj[...] = (pa[...] + pb[...]).astype(BF16)


def power_step(links, place, step, m):
    xf, xt, proj, yb, img, za, ga = (m[n] for n in ("xf", "xt", "proj", "yb", "img", "za", "ga"))
    t1, t2, mine = m["t1"], m["t2"], m["mine"]
    theirs, own_y = m["theirs"].at[step], m["y"].at[step]
    u, v, w = (place.coord[a] for a in "uvw")

    def image_slab(d):
        start = mo(((u + d + 4) % 4) * 512, 512)
        img[d % 4] = jnp.dot(xt[pl.ds(start, 512), :], proj[...], preferred_element_type=F32)
        return img.at[d % 4]

    scatter_stage(links, place, "u", image_slab, 512, BF16, m["bu"], t1)
    scatter_stage(
        links, place, "v", lambda d: t1.at[pl.ds(mo(((v + d + 4) % 4) * 128, 128), 128)], 128, F32, m["bv"], t2
    )
    scatter_stage(
        links, place, "w", lambda d: t2.at[pl.ds(mo(((w + d + 4) % 4) * 32, 32), 32)], 32, F32, m["bw"], m["t3"]
    )
    image = m["t3"][...] * (1.0 / ROWS)
    high = image.astype(BF16)
    own_y[:, 0:K] = high
    own_y[:, K : 2 * K] = (image - high.astype(F32)).astype(BF16)
    yb[pl.ds(mo((u * 16 + v * 4 + w) * 32, 32), 32), :] = own_y[...]

    def consume(d, first=False):
        slab = pl.ds(mo(((u + d + 4) % 4) * 512, 512), 512)
        term = jnp.dot(xf[:, slab], yb[slab, :], preferred_element_type=F32)
        za[...] = term if first else za[...] + term
        term = lax.dot_general(
            yb[slab, 0:K], yb[slab, :], (((0,), (0,)), ((), ())), preferred_element_type=F32
        )
        ga[...] = term if first else ga[...] + term

    first = True
    for ready in flood(links, place, yb, own_y):
        for d in ready or ():
            consume(d, first)
            first = False
    mine[0:512, :] = za[:, 0:K] + za[:, K : 2 * K]
    cross = ga[:, K : 2 * K]
    mine[512:1024, :] = ga[:, 0:K] + (cross + cross.T)
    swap = links.copy(links.slot(), mine, theirs, place.partner())
    swap.start()
    swap.wait()
    m["zs"][0:512, :] = mine[0:512, :] + theirs[0:512, :]
    m["s"][...] = mine[512:1024, :] + theirs[512:1024, :]


class UpDown:
    def __init__(self, links, place, ub, x, lo):
        self.links, self.ub, self.x, self.lo, self.z = links, ub, x, lo, place.z
        self.up, self.down = place.at(0, 0, 1, place.k), place.at(0, 0, -1, place.k)
        self.slots = [links.slot() for _ in range(4)]
        self.sent = []

    def part(self, d, lo=0, n=128):
        return self.ub.at[(self.z + d + 4) % 4, self.x, pl.ds(self.lo + lo, n)]

    def _send(self, i, ref, device):
        copy = self.links.copy(self.slots[i], ref, ref, device)
        copy.start()
        self.sent.append(copy)

    def start(self):
        self._send(0, self.part(0), self.up)
        self._send(1, self.part(0), self.down)

    def relay(self):
        self.links.arrived(self.slots[0], self.part(-1), self.up)
        self._send(2, self.part(-1, 0, 64), self.up)
        self.links.arrived(self.slots[1], self.part(1), self.up)
        self._send(3, self.part(1, 64, 64), self.down)

    def far(self):
        self.links.arrived(self.slots[2], self.part(2, 0, 64), self.up)
        self.links.arrived(self.slots[3], self.part(2, 64, 64), self.up)


def nearest_rows(links, place, limit, out, m):
    z, k, xl = place.z, place.k, place.x % 2
    units, ub, lb, labs, best, tops = (m[n] for n in ("units", "ub", "lb", "labs", "best", "tops"))
    across = place.at(1 - 2 * xl, 0, 0, k)
    ub[z, xl] = units[pl.ds(mo(k * 256, 256), 256), :]
    sent = []
    slots = [links.slot() for _ in range(5)]

    def cross(i, d, lo):
        ref = ub.at[(z + d + 4) % 4, xl, pl.ds(lo, 128)]
        copy = links.copy(slots[i], ref, ref, across)
        copy.start()
        sent.append(copy)

    def crossed(i, d, lo):
        links.arrived(slots[i], ub.at[(z + d + 4) % 4, 1 - xl, pl.ds(lo, 128)], across)

    ga = UpDown(links, place, ub, xl, 0)
    gb = UpDown(links, place, ub, xl, 128)
    gc = UpDown(links, place, ub, 1 - xl, 0)
    cross(0, 0, 0)
    gb.start()
    ga.start()
    cross(1, 0, 128)
    best[...] = jnp.full((512, 128), -1.0, F32)
    bound = limit[0:1, :]
    lane_id = lax.broadcasted_iota(jnp.int32, (1, 128), 1)
    own_first = (z * 4 + xl * 2) * 256

    def score(d, x):
        zz = (z + d + 4) % 4
        labels = lb[zz, x][0:1, :].astype(F32)
        first = (zz * 4 + x * 2 + k) * 256

        def part(r, n):
            value = lax.dot_general(units[pl.ds(r, n), :], ub[zz, x], TT, preferred_element_type=F32)
            rows = lax.broadcasted_iota(jnp.int32, (n, 128), 0) + (own_first + r)
            label = labs[pl.ds(r, n), :].astype(F32)
            top = best[pl.ds(r, n), :]
            for t in range(2):
                lanes = slice(t * 128, t * 128 + 128)
                other = lane_id + (first + t * 128)
                use = (label == labels[:, lanes]) & (other < bound) & (other != rows)
                top = jnp.maximum(top, jnp.where(use, value[:, lanes], -1.0))
            best[pl.ds(r, n), :] = top

        rows_loop(512, 256, part)

    score(0, xl)
    crossed(0, 0, 0)
    gc.start()
    gb.relay()
    cross(2, -1, 128)
    cross(3, 1, 128)
    ga.relay()
    gb.far()
    cross(4, 2, 128)

    def pair(i, carry):
        score(2 * i - 1, xl)
        return carry

    lax.fori_loop(0, 2, pair, 0)
    gc.relay()
    crossed(1, 0, 128)
    score(0, 1 - xl)
    ga.far()
    score(2, xl)
    crossed(2, -1, 128)
    crossed(3, 1, 128)

    def other_pair(i, carry):
        score(2 * i - 1, 1 - xl)
        return carry

    lax.fori_loop(0, 2, other_pair, 0)
    gc.far()
    crossed(4, 2, 128)
    score(2, 1 - xl)
    for copy in sent + ga.sent + gb.sent + gc.sent:
        copy.wait_send()
    top = jnp.max(best[...].T, axis=0, keepdims=True)
    tops[0] = jnp.broadcast_to(top, (8, 512))
    swap = links.copy(links.slot(), tops.at[0], tops.at[1], place.partner())
    swap.start()
    swap.wait()
    out[...] = jnp.maximum(tops[0], tops[1])


def whole_kernel(
    e_ref, sb_ref, s0_ref, s1_ref, lab_ref, row_ref, limit, subspace, nearest, send, recv, m
):
    links, place = Links(send, recv), Place()
    k, xl = place.k, place.x % 2
    devices = [place.along(a, d) for a in "uvw" for d in (1, -1, 2)] + [place.partner()]
    flip = 1 - 2 * xl
    devices += [place.at(flip, 0, dz, k) for dz in (1, 2, 3)]
    greet(devices)
    first_product(links, place, e_ref, sb_ref, s0_ref, s1_ref, lab_ref, row_ref, m)
    s, zs, out, ad, wp, lp = (m[n] for n in ("s", "zs", "out", "ad", "wp", "lp"))
    power_step(links, place, 0, m)
    factor_apply(s, zs, CHUNKS, out, ad, wp, lp)
    m["proj"][...] = out[0:512, :].astype(BF16)
    power_step(links, place, 1, m)
    own_y = m["y"].at[1]
    zs[512:544, :] = own_y[:, 0:K].astype(F32) + own_y[:, K : 2 * K].astype(F32)
    factor_apply(s, zs, CHUNKS + [(512, 32)], out, ad, wp, lp)
    units = m["units"]
    for i in range(4):
        coords = out[i * 128 : i * 128 + 128, :]
        size = jnp.sum(coords * coords, axis=1, keepdims=True) + EPS
        units[i * 128 : i * 128 + 128, :] = (coords * lax.rsqrt(size)).astype(BF16)
    subspace[...] = out[512:544, :] * math.sqrt(D)
    nearest_rows(links, place, limit, nearest, m)


def body(embeddings, start_basis, cluster_ids, valid_counts):
    labels = cluster_ids.astype(BF16)
    label_columns = jnp.broadcast_to(labels[:, None], (256, 128))
    label_rows = jnp.broadcast_to(labels[None, :], (16, 256))
    limit = jnp.broadcast_to(valid_counts[None, :], (8, 128))
    s0, s1 = selections()
    vmem = pl.BlockSpec(memory_space=pltpu.VMEM)
    slots = 256
    subspace, nearest = pl.pallas_call(
        whole_kernel,
        out_shape=[jax.ShapeDtypeStruct((32, K), F32), jax.ShapeDtypeStruct((8, 512), F32)],
        in_specs=[vmem] * 7,
        out_specs=[vmem] * 2,
        scratch_shapes=[pltpu.SemaphoreType.DMA((slots,)), pltpu.SemaphoreType.DMA((slots,)), SCRATCH],
        compiler_params=pltpu.CompilerParams(
            collective_id=0, has_side_effects=True, vmem_limit_bytes=VMEM_LIMIT
        ),
        name="whole",
    )(embeddings, start_basis, s0, s1, label_columns, label_rows, limit)
    core = lax.axis_index("member") % 2
    own = lax.dynamic_slice(nearest[0], (core * 256,), (256,))
    return (subspace, own)


def solution(mesh):
    placed = (
        P(("cluster", "member"), None),
        P(("cluster", "member"), None),
        P(("cluster", "member")),
        P("cluster"),
    )
    return jax.shard_map(
        body,
        mesh=mesh,
        in_specs=placed,
        out_specs=(P(("cluster", "member"), None), P(("cluster", "member"))),
        check_vma=False,
    )
```

```python
import functools
import math

import jax
import jax.numpy as jnp
import numpy as np
from jax import lax
from jax.experimental import pallas as pl
from jax.experimental.pallas import tpu as pltpu
from jax.sharding import PartitionSpec as P

EPS = 1e-06
MESH = pl.DeviceIdType.MESH
F32 = jnp.float32
BF16 = jnp.bfloat16
D = 4096
K = 512
ROWS = 32768
VMEM_LIMIT = 60 * 1024 * 1024


class Links:
    def __init__(self, send, recv):
        self.send, self.recv, self.used = send, recv, 0

    def slot(self):
        self.used += 1
        return self.used - 1

    def copy(self, slot, src, dst, device):
        return pltpu.make_async_remote_copy(
            src_ref=src,
            dst_ref=dst,
            send_sem=self.send.at[slot],
            recv_sem=self.recv.at[slot],
            device_id=device,
            device_id_type=MESH,
        )

    def arrived(self, slot, dst, device):
        self.copy(slot, dst, dst, device).wait_recv()


class Place:
    def __init__(self):
        c, m = lax.axis_index("cluster"), lax.axis_index("member")
        self.x = (c // 4) * 2 + (m // 2) % 2
        self.y = c % 4
        self.z = m // 4
        self.k = m % 2
        k, o = self.k, 1 - self.k
        self.coord = {
            "u": self.x * o + self.y * k,
            "v": self.z,
            "w": self.y * o + self.x * k,
        }

    def at(self, dx, dy, dz, core):
        x = (self.x + dx + 4) % 4
        y = (self.y + dy + 4) % 4
        z = (self.z + dz + 4) % 4
        return ((x // 2) * 4 + y, z * 4 + (x % 2) * 2 + core)

    def along(self, axis, d):
        k, o = self.k, 1 - self.k
        if axis == "u":
            return self.at(d * o, d * k, 0, k)
        if axis == "v":
            return self.at(0, 0, d, k)
        return self.at(d * k, d * o, 0, k)

    def partner(self):
        return self.at(0, 0, 0, 1 - self.k)


def greet(devices):
    barrier = pltpu.get_barrier_semaphore()
    for device in devices:
        pl.semaphore_signal(barrier, inc=1, device_id=device, device_id_type=MESH)
    pl.semaphore_wait(barrier, len(devices))


def mo(i, n):
    return pl.multiple_of(i, n)


class GatherStage:
    def __init__(self, links, place, axis, buf, base, n, stride, source=None):
        self.links, self.buf, self.n, self.h = links, buf, n, n // 2
        self.base, self.stride, self.coord = base, stride, place.coord[axis]
        self.plus, self.minus = place.along(axis, 1), place.along(axis, -1)
        self.slots = [links.slot() for _ in range(4)]
        self.source = source
        self.sent = []

    def region(self, d, part=None):
        start = mo(self.base + ((self.coord + d + 4) % 4) * self.stride, self.n)
        if part is None:
            return self.buf.at[pl.ds(start, self.n)]
        return self.buf.at[pl.ds(mo(start + part * self.h, self.h), self.h)]

    def _send(self, i, src, dst, device):
        copy = self.links.copy(self.slots[i], src, dst, device)
        copy.start()
        self.sent.append(copy)

    def start(self):
        own = self.region(0)
        src = own if self.source is None else self.source
        self._send(0, src, own, self.plus)
        self._send(1, src, own, self.minus)

    def relay(self):
        self.links.arrived(self.slots[0], self.region(-1), self.plus)
        first = self.region(-1, 0)
        self._send(2, first, first, self.plus)
        self.links.arrived(self.slots[1], self.region(1), self.plus)
        second = self.region(1, 1)
        self._send(3, second, second, self.minus)

    def far(self):
        self.links.arrived(self.slots[2], self.region(2, 0), self.plus)
        self.links.arrived(self.slots[3], self.region(2, 1), self.plus)

    def drain(self):
        for copy in self.sent:
            copy.wait_send()


class DirectStage(GatherStage):
    def __init__(self, links, place, axis, *rest, **more):
        super().__init__(links, place, axis, *rest, **more)
        self.opposite = place.along(axis, 2)

    def start(self):
        super().start()
        own = self.region(0)
        src = own if self.source is None else self.source
        self._send(2, src, own, self.opposite)

    def near(self):
        self.links.arrived(self.slots[0], self.region(-1), self.plus)
        self.links.arrived(self.slots[1], self.region(1), self.plus)

    def far(self):
        self.links.arrived(self.slots[2], self.region(2), self.plus)


def flood(links, place, buf, source):
    u, v, w = (place.coord[a] for a in "uvw")

    def ahead(c, d):
        return (c + d + 4) % 4

    own = {0: source}
    wst = DirectStage(links, place, "w", buf, (u * 16 + v * 4) * 32, 32, 32, source=source)
    vst = {
        e: GatherStage(links, place, "v", buf, u * 512 + ahead(w, e) * 32, 32, 128, source=own.get(e))
        for e in (0, -1, 1, 2)
    }
    ust = {
        e: GatherStage(links, place, "u", buf, v * 128 + ahead(w, e) * 32, 32, 512, source=own.get(e))
        for e in (0, -1, 1, 2)
    }
    big = {f: GatherStage(links, place, "u", buf, ahead(v, f) * 128, 128, 512) for f in (-1, 1, 2)}
    wst.start()
    vst[0].start()
    ust[0].start()
    yield None
    wst.near()
    for e in (-1, 1):
        vst[e].start()
        ust[e].start()
    vst[0].relay()
    ust[0].relay()
    yield None
    wst.far()
    vst[2].start()
    ust[2].start()
    for e in (-1, 1):
        vst[e].relay()
        ust[e].relay()
    yield None
    vst[2].relay()
    big[-1].start()
    big[1].start()
    ust[2].relay()
    for e in (0, -1, 1, 2):
        vst[e].far()
    big[2].start()
    yield (0,)
    for f in (-1, 1, 2):
        big[f].relay()
    yield (1, -1)
    for e in (0, -1, 1, 2):
        ust[e].far()
    for f in (-1, 1, 2):
        big[f].far()
    yield (2,)
    for stage in [wst, *vst.values(), *ust.values(), *big.values()]:
        stage.drain()


def rows_loop(total, step, fn):
    if total <= step:
        fn(0, total)
        return

    def body(i, carry):
        fn(mo(i * step, step), step)
        return carry

    lax.fori_loop(0, total // step, body, 0)


class ScatterStage:
    def __init__(self, links, place, axis, term, n, dtype, bufs):
        self.links, self.term, self.h, self.dtype = links, term, n // 2, dtype
        self.s2, self.sp, self.sm, self.ra, self.rb, self.rp, self.rm = bufs
        self.plus, self.minus = place.along(axis, 1), place.along(axis, -1)
        self.slots = [links.slot() for _ in range(6)]
        self.low, self.high = pl.ds(0, n // 2), pl.ds(n // 2, n // 2)
        self.sent = []

    def _send(self, i, src, dst, device):
        copy = self.links.copy(self.slots[i], src, dst, device)
        copy.start()
        self.sent.append(copy)

    def _got(self, i, dst):
        self.links.arrived(self.slots[i], dst, self.plus)

    def send_far(self):
        self.s2[...] = self.term(2)[...].astype(self.dtype)
        self._send(0, self.s2.at[self.low], self.ra, self.plus)
        self._send(1, self.s2.at[self.high], self.rb, self.minus)

    def send_plus(self):
        self.sp[self.high, :] = self.term(1)[self.high, :].astype(self.dtype)
        self._send(2, self.sp.at[self.high], self.rp.at[self.high], self.plus)

    def send_minus(self):
        self.sm[self.low, :] = self.term(-1)[self.low, :].astype(self.dtype)
        self._send(3, self.sm.at[self.low], self.rm.at[self.low], self.minus)

    def relay(self):
        self._got(0, self.ra)
        self.sp[self.low, :] = (self.term(1)[self.low, :] + self.ra[...].astype(F32)).astype(self.dtype)
        self._send(4, self.sp.at[self.low], self.rp.at[self.low], self.plus)
        self._got(1, self.rb)
        self.sm[self.high, :] = (self.term(-1)[self.high, :] + self.rb[...].astype(F32)).astype(self.dtype)
        self._send(5, self.sm.at[self.high], self.rm.at[self.high], self.minus)

    def finish(self, out):
        self._got(2, self.rp.at[self.high])
        self._got(3, self.rm.at[self.low])
        self._got(4, self.rp.at[self.low])
        self._got(5, self.rm.at[self.high])
        out[...] = self.term(0)[...] + (self.rp[...].astype(F32) + self.rm[...].astype(F32))

    def drain(self):
        for copy in self.sent:
            copy.wait_send()


def reduce_image(links, place, image_slab, m):
    u, v, w = (place.coord[a] for a in "uvw")
    t1, t2, from_w = m["t1"], m["t2"], m["bw"]

    def slab(c, d, n):
        return pl.ds(mo(((c + d + 4) % 4) * n, n), n)

    images = {}

    def piece(i, f):
        rows = slab(v, f, 128)
        full, half = pl.ds(i * 128, 128), pl.ds(i * 64, 64)
        bufs = [ref.at[half if j in (3, 4) else full] for j, ref in enumerate(m["bu"])]
        return ScatterStage(links, place, "u", lambda d: images[d].at[rows], 128, BF16, bufs)

    far, plus, minus, own = (piece(i, f) for i, f in enumerate((2, 1, -1, 0)))
    down = ScatterStage(links, place, "v", lambda d: t1.at[slab(v, d, 128)], 128, F32, m["bv"])

    def start(stage):
        stage.send_far()
        stage.send_plus()
        stage.send_minus()

    images[2] = image_slab(2)
    far.send_far()
    images[1] = image_slab(1)
    images[-1] = image_slab(-1)
    far.send_plus()
    far.send_minus()
    start(plus)
    images[0] = image_slab(0)
    far.relay()
    start(minus)
    plus.relay()
    start(own)
    far.finish(t1.at[slab(v, 2, 128)])
    down.send_far()
    minus.relay()
    plus.finish(t1.at[slab(v, 1, 128)])
    down.send_plus()
    own.relay()
    minus.finish(t1.at[slab(v, -1, 128)])
    down.send_minus()
    down.relay()
    own.finish(t1.at[slab(v, 0, 128)])
    down.finish(t2)
    copies = []
    for i, d in enumerate((1, -1, 2)):
        copy = links.copy(links.slot(), t2.at[slab(w, d, 32)], from_w.at[i], place.along("w", d))
        copy.start()
        copies.append(copy)
    for copy in copies:
        copy.wait()
    for stage in (far, plus, minus, own, down):
        stage.drain()
    return t2[slab(w, 0, 32), :] + ((from_w[0] + from_w[1]) + from_w[2])


def sub(x, c):
    return jnp.broadcast_to(x[c : c + 1, :], (8, 128))


def lane(x, j):
    return jnp.broadcast_to(x[:, j : j + 1], (8, 128))


HIGH = lax.Precision.HIGHEST
TT = (((1,), (1,)), ((), ()))


def dot6(a, b):
    return lax.dot_general(a, b, TT, precision=HIGH, preferred_element_type=F32)


def split(a):
    high = a.astype(BF16)
    return high, (a - high.astype(F32)).astype(BF16)


def dot3(a, b):
    def one(p, q):
        return lax.dot_general(p, q, TT, preferred_element_type=F32)

    return one(a[0], b[0]) + (one(a[0], b[1]) + one(a[1], b[0]))


def inverse_factor_128(a_rows, w_rows, between):
    row_id = lax.broadcasted_iota(jnp.int32, (8, 128), 0)
    out = []
    for p in range(16):
        j0 = 8 * p
        va, vw = a_rows[p], w_rows[p]
        diag = [lane(va, j0 + b) for b in range(8)]
        tops, inverses, pivots, rows = [], [], [], []
        for c in range(8):
            pivot = sub(diag[c], c)
            q = 1.0 / pivot
            f = jnp.where(row_id > c, diag[c] * q, 0.0)
            ua, uw = sub(va, c), sub(vw, c)
            row = {b: sub(diag[b], c) for b in range(c + 1, 8)}
            va, vw = va - f * ua, vw - f * uw
            for b in range(c + 1, 8):
                diag[b] = diag[b] - f * row[b]
            tops.append((ua, uw))
            inverses.append(q)
            pivots.append(pivot)
            rows.append(row)
        scale = pivots[0]
        for c in range(1, 8):
            scale = jnp.where(row_id == c, pivots[c], scale)
        out.append(vw * lax.rsqrt(scale))
        for i in range(p + 1, 16):
            below = [lane(a_rows[i], j0 + b) for b in range(8)]
            a, w = a_rows[i], w_rows[i]
            for c in range(8):
                f = below[c] * inverses[c]
                a, w = a - f * tops[c][0], w - f * tops[c][1]
                for b in range(c + 1, 8):
                    below[b] = below[b] - f * rows[c][b]
            a_rows[i], w_rows[i] = a, w
        between(p)
    return out


def factor_apply(s, zs, chunks, out, ad, wp, lp, fill):
    row_id = lax.broadcasted_iota(jnp.int32, (8, 128), 0)
    lane_id = lax.broadcasted_iota(jnp.int32, (8, 128), 1)
    ad[...] = s[0:128, 0:128]
    wp[...] = jnp.zeros((128, 128), F32)
    lp[...] = jnp.zeros((512, 128), F32)

    def step(kb, carry):
        prev = pl.ds(mo(jnp.maximum(kb - 1, 0) * 128, 128), 128)
        col = pl.ds(mo(kb * 128, 128), 128)
        a_rows = [ad[8 * i : 8 * i + 8, :] for i in range(16)]
        w_rows = [jnp.where(lane_id == row_id + 8 * i, 1.0, 0.0) for i in range(16)]
        inverse = split(wp[...])

        def gram_chunk(i):
            r = slice(i * 128, i * 128 + 128)
            s[r, :] = s[r, :] - dot6(lp[r, :], lp[...])

        def row_chunk(lo, n):
            r = slice(lo, lo + n)
            c = dot3(split(zs[r, prev]), inverse)
            out[r, prev] = c
            zs[r, :] = zs[r, :] - dot3(split(c), split(lp[...]))

        work = [functools.partial(gram_chunk, i) for i in range(4)]
        work += [functools.partial(row_chunk, lo, n) for lo, n in chunks]

        def between(p):
            if p % 2 == 1 and work:
                work.pop(0)()
            while p == 15 and work:
                work.pop(0)()

        rows = inverse_factor_128(a_rows, w_rows, between)
        for i in range(16):
            wp[8 * i : 8 * i + 8, :] = rows[i]
        new = dot6(s[:, col], wp[...])
        below = lax.broadcasted_iota(jnp.int32, (512, 128), 0) >= (kb + 1) * 128
        lp[...] = jnp.where(below, new, 0.0)
        following = pl.ds(mo(jnp.minimum(kb + 1, 3) * 128, 128), 128)
        ad[...] = s[following, following] - dot6(lp[following, :], lp[following, :])

        @pl.when(kb == 0)
        def _():
            fill()

        return carry

    lax.fori_loop(0, 4, step, 0)
    inverse = split(wp[...])
    for lo, n in chunks:
        out[lo : lo + n, 384:512] = dot3(split(zs[lo : lo + n, 384:512]), inverse)


def selections():
    s0 = np.zeros((2, 512, 128), np.float32)
    s1 = np.zeros((2, 128, 128), np.float32)
    r = np.arange(32)
    for lo in range(2):
        for y in range(4):
            s0[lo, y * 128 + lo * 64 + r, y * 32 + r] = 1
        for hi in range(2):
            s1[hi, (lo * 2 + 1) * 32 + r, (hi * 2 + lo) * 32 + r] = 1
    return jnp.asarray(s0, BF16), jnp.asarray(s1, BF16)


def bands(n, dtype):
    h = n // 2
    shapes = [(n, K), (n, K), (n, K), (h, K), (h, K), (n, K), (n, K)]
    return [pltpu.VMEM(shape, dtype) for shape in shapes]


CHUNKS = [(i * 128, 128) for i in range(4)]
SCRATCH = {
    "packed": pltpu.VMEM((2, 256, 2048), BF16),
    "raw": pltpu.VMEM((512, 2048), BF16),
    "xf": pltpu.VMEM((512, 2048), BF16),
    "xt": pltpu.VMEM((2048, 512), BF16),
    "b0": pltpu.VMEM((2048, K), BF16),
    "sums": pltpu.VMEM((3, 4, 8, 2048), F32),
    "pa": pltpu.VMEM((512, K), F32),
    "pb": pltpu.VMEM((512, K), F32),
    "proj": pltpu.VMEM((512, K), BF16),
    "y": pltpu.VMEM((2, 32, 2 * K), BF16),
    "yb": pltpu.VMEM((2048, 2 * K), BF16),
    "img": pltpu.VMEM((4, 512, K), F32),
    "t1": pltpu.VMEM((512, K), F32),
    "t2": pltpu.VMEM((128, K), F32),
    "za": pltpu.VMEM((512, 2 * K), F32),
    "ga": pltpu.VMEM((512, 2 * K), F32),
    "mine": pltpu.VMEM((1024, K), F32),
    "theirs": pltpu.VMEM((2, 1024, K), F32),
    "bu": bands(512, BF16),
    "bv": bands(128, F32),
    "bw": pltpu.VMEM((3, 32, K), F32),
    "s": pltpu.VMEM((512, 512), F32),
    "zs": pltpu.VMEM((544, 512), F32),
    "out": pltpu.VMEM((544, 512), F32),
    "ad": pltpu.VMEM((128, 128), F32),
    "wp": pltpu.VMEM((128, 128), F32),
    "lp": pltpu.VMEM((512, 128), F32),
    "labs": pltpu.VMEM((512, 128), BF16),
    "lb": pltpu.VMEM((4, 2, 16, 256), BF16),
    "units": pltpu.VMEM((512, K), BF16),
    "ub": pltpu.VMEM((4, 2, 256, K), BF16),
    "best": pltpu.VMEM((512, 128), F32),
    "tops": pltpu.VMEM((2, 8, 512), F32),
}


def first_product(links, place, e_ref, sb_ref, s0_ref, s1_ref, ids_ref, m):
    u, v, w, k = (*(place.coord[a] for a in "uvw"), place.k)
    z, xl = place.z, place.x % 2
    partner = place.partner()
    packed, raw, xf, xt, b0, sums = (m[n] for n in ("packed", "raw", "xf", "xt", "b0", "sums"))
    gather = flood(links, place, b0, sb_ref)
    next(gather)
    b0[pl.ds(mo((u * 16 + v * 4 + w) * 32, 32), 32), :] = sb_ref[...]

    def pack(t, carry):
        x, q = t // 4, t % 4
        tiles = [e_ref[:, pl.ds(mo((((x // 2) * 4 + y) * 4 + q) * 128, 128), 128)] for y in range(4)]
        lanes = pl.ds(mo(t * 128, 128), 128)
        packed[0, :, lanes] = jnp.dot(
            jnp.concatenate(tiles, axis=1), s0_ref[x % 2], preferred_element_type=F32
        ).astype(BF16)
        near = jnp.dot(e_ref[:, lanes], s1_ref[0], preferred_element_type=F32)
        far = jnp.dot(e_ref[:, pl.ds(mo(2048 + t * 128, 128), 128)], s1_ref[1], preferred_element_type=F32)
        packed[1, :, lanes] = (near + far).astype(BF16)
        return carry

    lax.fori_loop(0, 16, pack, 0, unroll=4)
    mine = pl.ds(mo(k * 256, 256), 256)
    swap_rows = links.copy(links.slot(), packed.at[1 - k], raw.at[mine], partner)
    swap_rows.start()
    raw[mine, :] = packed[k]
    labs, lb = m["labs"], m["lb"]
    ids = jnp.broadcast_to(ids_ref[...].astype(F32), (128, 256))
    labs[mine, :] = ids.T.astype(BF16)
    lb[z, xl] = ids[0:16, :].astype(BF16)
    small = [links.copy(links.slot(), labs.at[mine], labs.at[mine], partner)]
    for dz in range(4):
        for dx in range(2):
            if dz or dx:
                device = place.at(dx * (1 - 2 * xl), 0, dz, k)
                small.append(links.copy(links.slot(), lb.at[z, xl], lb.at[z, xl], device))
    for copy in small:
        copy.start()
    next(gather)
    swap_rows.wait()

    def exchange(stage, axis, value):
        here = place.coord[axis]
        sums[stage, here] = value
        copies = []
        for d in (1, -1, 2):
            copy = links.copy(links.slot(), sums.at[stage, here], sums.at[stage, here], place.along(axis, d))
            copy.start()
            copies.append(copy)

        def done():
            for copy in copies:
                copy.wait()
            return (sums[stage, 0] + sums[stage, 1]) + (sums[stage, 2] + sums[stage, 3])

        return done

    done = exchange(0, "u", jnp.dot(jnp.ones((8, 512), BF16), raw[...], preferred_element_type=F32))
    next(gather)
    done = exchange(1, "v", done())
    next(gather)
    done = exchange(2, "w", done())
    average = done()[0:1, :] / ROWS

    def center(r, n):
        xf[pl.ds(r, n), :] = (raw[pl.ds(r, n), :].astype(F32) - average).astype(BF16)

    rows_loop(512, 32, center)

    def turn(t, carry):
        lanes = pl.ds(mo(t * 128, 128), 128)
        xt[lanes, :] = xf[:, lanes].T
        return carry

    lax.fori_loop(0, 16, turn, 0)
    pa, pb, proj = m["pa"], m["pb"], m["proj"]

    def product(d, first=False):
        slab = pl.ds(mo(((u + d + 4) % 4) * 512, 512), 512)
        term = jnp.dot(xf[:, slab], b0[slab, :], preferred_element_type=F32)
        pa[...] = term if first else pa[...] + term

    product(0, first=True)
    next(gather)
    product(1)
    product(-1)
    next(gather)
    product(2)
    next(gather, None)
    swap = links.copy(links.slot(), pa, pb, partner)
    swap.start()
    for copy in small:
        copy.wait()
    swap.wait()
    proj[...] = (pa[...] + pb[...]).astype(BF16)


def power_step(links, place, step, m):
    xf, xt, proj, yb, img, za, ga = (m[n] for n in ("xf", "xt", "proj", "yb", "img", "za", "ga"))
    mine, theirs, own_y = m["mine"], m["theirs"].at[step], m["y"].at[step]
    u, v, w = (place.coord[a] for a in "uvw")

    def image_slab(d):
        start = mo(((u + d + 4) % 4) * 512, 512)
        img[d % 4] = jnp.dot(xt[pl.ds(start, 512), :], proj[...], preferred_element_type=F32)
        return img.at[d % 4]

    image = reduce_image(links, place, image_slab, m) * (1.0 / ROWS)
    high = image.astype(BF16)
    own_y[:, 0:K] = high
    own_y[:, K : 2 * K] = (image - high.astype(F32)).astype(BF16)
    yb[pl.ds(mo((u * 16 + v * 4 + w) * 32, 32), 32), :] = own_y[...]

    def slab(d):
        return pl.ds(mo(((u + d + 4) % 4) * 512, 512), 512)

    def gram(d, first=False):
        term = lax.dot_general(
            yb[slab(d), 0:K], yb[slab(d), :], (((0,), (0,)), ((), ())), preferred_element_type=F32
        )
        ga[...] = term if first else ga[...] + term

    def product(d, first=False):
        term = jnp.dot(xf[:, slab(d)], yb[slab(d), :], preferred_element_type=F32)
        za[...] = term if first else za[...] + term

    gather = flood(links, place, yb, own_y)
    for ready in gather:
        if ready == (2,):
            break
        for d in ready or ():
            gram(d, d == 0)
            product(d, d == 0)
    partner = place.partner()
    top, bottom = pl.ds(0, 512), pl.ds(512, 512)
    gram(2)
    cross = ga[:, K : 2 * K]
    mine[bottom, :] = ga[:, 0:K] + (cross + cross.T)
    swap_gram = links.copy(links.slot(), mine.at[bottom], theirs.at[bottom], partner)
    swap_gram.start()
    product(2)
    mine[top, :] = za[:, 0:K] + za[:, K : 2 * K]
    swap_rows = links.copy(links.slot(), mine.at[top], theirs.at[top], partner)
    swap_rows.start()
    next(gather, None)
    swap_gram.wait()
    m["s"][...] = mine[bottom, :] + theirs[bottom, :]

    def fill():
        swap_rows.wait()
        m["zs"][0:512, :] = mine[top, :] + theirs[top, :]

    return fill


class UpDown:
    def __init__(self, links, place, ub, x, lo):
        self.links, self.ub, self.x, self.lo, self.z = links, ub, x, lo, place.z
        self.up, self.down = place.at(0, 0, 1, place.k), place.at(0, 0, -1, place.k)
        self.slots = [links.slot() for _ in range(4)]
        self.sent = []

    def part(self, d, lo=0, n=128):
        return self.ub.at[(self.z + d + 4) % 4, self.x, pl.ds(self.lo + lo, n)]

    def _send(self, i, ref, device):
        copy = self.links.copy(self.slots[i], ref, ref, device)
        copy.start()
        self.sent.append(copy)

    def start(self):
        self._send(0, self.part(0), self.up)
        self._send(1, self.part(0), self.down)

    def relay(self):
        self.links.arrived(self.slots[0], self.part(-1), self.up)
        self._send(2, self.part(-1, 0, 64), self.up)
        self.links.arrived(self.slots[1], self.part(1), self.up)
        self._send(3, self.part(1, 64, 64), self.down)

    def far(self):
        self.links.arrived(self.slots[2], self.part(2, 0, 64), self.up)
        self.links.arrived(self.slots[3], self.part(2, 64, 64), self.up)


def nearest_rows(links, place, limit, out, m):
    z, k, xl = place.z, place.k, place.x % 2
    units, ub, lb, labs, best, tops = (m[n] for n in ("units", "ub", "lb", "labs", "best", "tops"))
    across = place.at(1 - 2 * xl, 0, 0, k)
    ub[z, xl] = units[pl.ds(mo(k * 256, 256), 256), :]
    sent = []
    slots = [links.slot() for _ in range(5)]

    def cross(i, d, lo):
        ref = ub.at[(z + d + 4) % 4, xl, pl.ds(lo, 128)]
        copy = links.copy(slots[i], ref, ref, across)
        copy.start()
        sent.append(copy)

    def crossed(i, d, lo):
        links.arrived(slots[i], ub.at[(z + d + 4) % 4, 1 - xl, pl.ds(lo, 128)], across)

    ga = UpDown(links, place, ub, xl, 0)
    gb = UpDown(links, place, ub, xl, 128)
    gc = UpDown(links, place, ub, 1 - xl, 0)
    cross(0, 0, 0)
    gb.start()
    ga.start()
    cross(1, 0, 128)
    best[...] = jnp.full((512, 128), -1.0, F32)
    bound = limit[0]
    lane_id = lax.broadcasted_iota(jnp.int32, (1, 128), 1)
    own_first = (z * 4 + xl * 2) * 256

    def score(d, x):
        zz = (z + d + 4) % 4
        labels = lb[zz, x][0:1, :].astype(F32)
        first = (zz * 4 + x * 2 + k) * 256

        def part(r, n):
            value = lax.dot_general(units[pl.ds(r, n), :], ub[zz, x], TT, preferred_element_type=F32)
            rows = lax.broadcasted_iota(jnp.int32, (n, 128), 0) + (own_first + r)
            label = labs[pl.ds(r, n), :].astype(F32)
            top = best[pl.ds(r, n), :]
            for t in range(2):
                lanes = slice(t * 128, t * 128 + 128)
                other = lane_id + (first + t * 128)
                use = (label == labels[:, lanes]) & (other < bound) & (other != rows)
                top = jnp.maximum(top, jnp.where(use, value[:, lanes], -1.0))
            best[pl.ds(r, n), :] = top

        rows_loop(512, 256, part)

    score(0, xl)
    crossed(0, 0, 0)
    gc.start()
    gb.relay()
    cross(2, -1, 128)
    cross(3, 1, 128)
    ga.relay()
    gb.far()
    cross(4, 2, 128)

    def pair(i, carry):
        score(2 * i - 1, xl)
        return carry

    lax.fori_loop(0, 2, pair, 0)
    gc.relay()
    crossed(1, 0, 128)
    score(0, 1 - xl)
    ga.far()
    score(2, xl)
    crossed(2, -1, 128)
    crossed(3, 1, 128)

    def other_pair(i, carry):
        score(2 * i - 1, 1 - xl)
        return carry

    lax.fori_loop(0, 2, other_pair, 0)
    gc.far()
    crossed(4, 2, 128)
    score(2, 1 - xl)
    for copy in sent + ga.sent + gb.sent + gc.sent:
        copy.wait_send()
    top = jnp.max(best[...].T, axis=0, keepdims=True)
    tops[0] = jnp.broadcast_to(top, (8, 512))
    swap = links.copy(links.slot(), tops.at[0], tops.at[1], place.partner())
    swap.start()
    swap.wait()
    top = jnp.maximum(tops[0], tops[1])[0:1, :]
    out[...] = jnp.where(k == 0, top[:, 0:256], top[:, 256:512])


def whole_kernel(
    e_ref, sb_ref, s0_ref, s1_ref, ids_ref, limit, subspace, nearest, send, recv, m
):
    links, place = Links(send, recv), Place()
    k, xl = place.k, place.x % 2
    devices = [place.along(a, d) for a in "uvw" for d in (1, -1, 2)] + [place.partner()]
    flip = 1 - 2 * xl
    devices += [place.at(flip, 0, dz, k) for dz in (1, 2, 3)]
    greet(devices)
    first_product(links, place, e_ref, sb_ref, s0_ref, s1_ref, ids_ref, m)
    s, zs, out, ad, wp, lp = (m[n] for n in ("s", "zs", "out", "ad", "wp", "lp"))
    fill = power_step(links, place, 0, m)
    factor_apply(s, zs, CHUNKS, out, ad, wp, lp, fill)
    m["proj"][...] = out[0:512, :].astype(BF16)
    fill = power_step(links, place, 1, m)
    own_y = m["y"].at[1]
    zs[512:544, :] = own_y[:, 0:K].astype(F32) + own_y[:, K : 2 * K].astype(F32)
    factor_apply(s, zs, CHUNKS + [(512, 32)], out, ad, wp, lp, fill)
    units = m["units"]
    for i in range(4):
        coords = out[i * 128 : i * 128 + 128, :]
        size = jnp.sum(coords * coords, axis=1, keepdims=True) + EPS
        units[i * 128 : i * 128 + 128, :] = (coords * lax.rsqrt(size)).astype(BF16)
    subspace[...] = out[512:544, :] * math.sqrt(D)
    nearest_rows(links, place, limit, nearest, m)


def body(embeddings, start_basis, cluster_ids, valid_counts):
    s0, s1 = selections()
    vmem = pl.BlockSpec(memory_space=pltpu.VMEM)
    slots = 256
    subspace, nearest = pl.pallas_call(
        whole_kernel,
        out_shape=[jax.ShapeDtypeStruct((32, K), F32), jax.ShapeDtypeStruct((1, 256), F32)],
        in_specs=[vmem] * 5 + [pl.BlockSpec(memory_space=pltpu.SMEM)],
        out_specs=[vmem] * 2,
        scratch_shapes=[pltpu.SemaphoreType.DMA((slots,)), pltpu.SemaphoreType.DMA((slots,)), SCRATCH],
        compiler_params=pltpu.CompilerParams(
            collective_id=0, has_side_effects=True, vmem_limit_bytes=VMEM_LIMIT
        ),
        name="whole",
    )(embeddings, start_basis, s0, s1, cluster_ids.reshape(1, 256), valid_counts)
    return (subspace, nearest.reshape(256))


def solution(mesh):
    placed = (
        P(("cluster", "member"), None),
        P(("cluster", "member"), None),
        P(("cluster", "member")),
        P("cluster"),
    )
    return jax.shard_map(
        body,
        mesh=mesh,
        in_specs=placed,
        out_specs=(P(("cluster", "member"), None), P(("cluster", "member"))),
        check_vma=False,
    )
```

```python
import functools
import math

import jax
import jax.numpy as jnp
import numpy as np
from jax import lax
from jax.experimental import pallas as pl
from jax.experimental.pallas import tpu as pltpu
from jax.sharding import PartitionSpec as P

EPS = 1e-06
MESH = pl.DeviceIdType.MESH
F32 = jnp.float32
BF16 = jnp.bfloat16
D = 4096
K = 512
ROWS = 32768
VMEM_LIMIT = 60 * 1024 * 1024
SLOTS = 272


class Links:
    def __init__(self, send, recv):
        self.send, self.recv, self.used = send, recv, 0

    def slot(self):
        self.used += 1
        return self.used - 1

    def copy(self, slot, src, dst, device):
        return pltpu.make_async_remote_copy(
            src_ref=src,
            dst_ref=dst,
            send_sem=self.send.at[slot],
            recv_sem=self.recv.at[slot],
            device_id=device,
            device_id_type=MESH,
        )

    def arrived(self, slot, dst, device):
        self.copy(slot, dst, dst, device).wait_recv()


class Place:
    def __init__(self):
        c, m = lax.axis_index("cluster"), lax.axis_index("member")
        self.x = (c // 4) * 2 + (m // 2) % 2
        self.y = c % 4
        self.z = m // 4
        self.k = m % 2
        k, o = self.k, 1 - self.k
        self.coord = {
            "u": self.x * o + self.y * k,
            "v": self.z,
            "w": self.y * o + self.x * k,
        }

    def at(self, dx, dy, dz, core):
        x = (self.x + dx + 4) % 4
        y = (self.y + dy + 4) % 4
        z = (self.z + dz + 4) % 4
        return ((x // 2) * 4 + y, z * 4 + (x % 2) * 2 + core)

    def along(self, axis, d):
        k, o = self.k, 1 - self.k
        if axis == "u":
            return self.at(d * o, d * k, 0, k)
        if axis == "v":
            return self.at(0, 0, d, k)
        return self.at(d * k, d * o, 0, k)

    def in_plane(self, dv, dw):
        return self.at(dw * self.k, dw * (1 - self.k), dv, self.k)

    def partner(self):
        return self.at(0, 0, 0, 1 - self.k)


def greet(devices):
    barrier = pltpu.get_barrier_semaphore()
    for device in devices:
        pl.semaphore_signal(barrier, inc=1, device_id=device, device_id_type=MESH)
    pl.semaphore_wait(barrier, len(devices))


def mo(i, n):
    return pl.multiple_of(i, n)


class GatherStage:
    def __init__(self, links, place, axis, buf, base, n, stride, source=None):
        self.links, self.buf, self.n, self.h = links, buf, n, n // 2
        self.base, self.stride, self.coord = base, stride, place.coord[axis]
        self.plus, self.minus = place.along(axis, 1), place.along(axis, -1)
        self.slots = [links.slot() for _ in range(4)]
        self.source = source
        self.sent = []

    def region(self, d, part=None):
        start = mo(self.base + ((self.coord + d + 4) % 4) * self.stride, self.n)
        if part is None:
            return self.buf.at[pl.ds(start, self.n)]
        return self.buf.at[pl.ds(mo(start + part * self.h, self.h), self.h)]

    def _send(self, i, src, dst, device):
        copy = self.links.copy(self.slots[i], src, dst, device)
        copy.start()
        self.sent.append(copy)

    def start(self):
        own = self.region(0)
        src = own if self.source is None else self.source
        self._send(0, src, own, self.plus)
        self._send(1, src, own, self.minus)

    def relay(self):
        self.links.arrived(self.slots[0], self.region(-1), self.plus)
        first = self.region(-1, 0)
        self._send(2, first, first, self.plus)
        self.links.arrived(self.slots[1], self.region(1), self.plus)
        second = self.region(1, 1)
        self._send(3, second, second, self.minus)

    def far(self):
        self.links.arrived(self.slots[2], self.region(2, 0), self.plus)
        self.links.arrived(self.slots[3], self.region(2, 1), self.plus)

    def drain(self):
        for copy in self.sent:
            copy.wait_send()


class DirectStage(GatherStage):
    def __init__(self, links, place, axis, *rest, **more):
        super().__init__(links, place, axis, *rest, **more)
        self.opposite = place.along(axis, 2)

    def start(self):
        super().start()
        own = self.region(0)
        src = own if self.source is None else self.source
        self._send(2, src, own, self.opposite)

    def near(self):
        self.links.arrived(self.slots[0], self.region(-1), self.plus)
        self.links.arrived(self.slots[1], self.region(1), self.plus)

    def far(self):
        self.links.arrived(self.slots[2], self.region(2), self.plus)


def flood(links, place, buf, source):
    u, v, w = (place.coord[a] for a in "uvw")

    def ahead(c, d):
        return (c + d + 4) % 4

    own = {0: source}
    wst = DirectStage(links, place, "w", buf, (u * 16 + v * 4) * 32, 32, 32, source=source)
    vst = {
        e: GatherStage(links, place, "v", buf, u * 512 + ahead(w, e) * 32, 32, 128, source=own.get(e))
        for e in (0, -1, 1, 2)
    }
    ust = {
        e: GatherStage(links, place, "u", buf, v * 128 + ahead(w, e) * 32, 32, 512, source=own.get(e))
        for e in (0, -1, 1, 2)
    }
    big = {f: GatherStage(links, place, "u", buf, ahead(v, f) * 128, 128, 512) for f in (-1, 1, 2)}
    wst.start()
    vst[0].start()
    ust[0].start()
    yield None
    wst.near()
    for e in (-1, 1):
        vst[e].start()
        ust[e].start()
    vst[0].relay()
    ust[0].relay()
    yield None
    wst.far()
    vst[2].start()
    ust[2].start()
    for e in (-1, 1):
        vst[e].relay()
        ust[e].relay()
    yield None
    vst[2].relay()
    big[-1].start()
    big[1].start()
    ust[2].relay()
    for e in (0, -1, 1, 2):
        vst[e].far()
    big[2].start()
    yield (0,)
    for f in (-1, 1, 2):
        big[f].relay()
    yield (1, -1)
    for e in (0, -1, 1, 2):
        ust[e].far()
    for f in (-1, 1, 2):
        big[f].far()
    yield (2,)
    for stage in [wst, *vst.values(), *ust.values(), *big.values()]:
        stage.drain()


def rows_loop(total, step, fn):
    if total <= step:
        fn(0, total)
        return

    def body(i, carry):
        fn(mo(i * step, step), step)
        return carry

    lax.fori_loop(0, total // step, body, 0)


class ScatterStage:
    def __init__(self, links, place, axis, term, n, dtype, bufs):
        self.links, self.term, self.h, self.dtype = links, term, n // 2, dtype
        self.s2, self.sp, self.sm, self.ra, self.rb, self.rp, self.rm = bufs
        self.plus, self.minus = place.along(axis, 1), place.along(axis, -1)
        self.slots = [links.slot() for _ in range(6)]
        self.low, self.high = pl.ds(0, n // 2), pl.ds(n // 2, n // 2)
        self.sent = []

    def _send(self, i, src, dst, device):
        copy = self.links.copy(self.slots[i], src, dst, device)
        copy.start()
        self.sent.append(copy)

    def _got(self, i, dst):
        self.links.arrived(self.slots[i], dst, self.plus)

    def send_far(self):
        self.s2[...] = self.term(2)[...].astype(self.dtype)
        self._send(0, self.s2.at[self.low], self.ra, self.plus)
        self._send(1, self.s2.at[self.high], self.rb, self.minus)

    def send_plus(self):
        self.sp[self.high, :] = self.term(1)[self.high, :].astype(self.dtype)
        self._send(2, self.sp.at[self.high], self.rp.at[self.high], self.plus)

    def send_minus(self):
        self.sm[self.low, :] = self.term(-1)[self.low, :].astype(self.dtype)
        self._send(3, self.sm.at[self.low], self.rm.at[self.low], self.minus)

    def relay(self):
        self._got(0, self.ra)
        self.sp[self.low, :] = (self.term(1)[self.low, :] + self.ra[...].astype(F32)).astype(self.dtype)
        self._send(4, self.sp.at[self.low], self.rp.at[self.low], self.plus)
        self._got(1, self.rb)
        self.sm[self.high, :] = (self.term(-1)[self.high, :] + self.rb[...].astype(F32)).astype(self.dtype)
        self._send(5, self.sm.at[self.high], self.rm.at[self.high], self.minus)

    def finish(self, out):
        self._got(2, self.rp.at[self.high])
        self._got(3, self.rm.at[self.low])
        self._got(4, self.rp.at[self.low])
        self._got(5, self.rm.at[self.high])
        out[...] = self.term(0)[...] + (self.rp[...].astype(F32) + self.rm[...].astype(F32))

    def drain(self):
        for copy in self.sent:
            copy.wait_send()


def reduce_image(links, place, image_slab, m):
    u, v, w = (place.coord[a] for a in "uvw")
    t1, t2, from_w = m["t1"], m["t2"], m["bw"]

    def slab(c, d, n):
        return pl.ds(mo(((c + d + 4) % 4) * n, n), n)

    images = {}

    def piece(i, f):
        rows = slab(v, f, 128)
        full, half = pl.ds(i * 128, 128), pl.ds(i * 64, 64)
        bufs = [ref.at[half if j in (3, 4) else full] for j, ref in enumerate(m["bu"])]
        return ScatterStage(links, place, "u", lambda d: images[d].at[rows], 128, BF16, bufs)

    far, plus, minus, own = (piece(i, f) for i, f in enumerate((2, 1, -1, 0)))
    down = ScatterStage(links, place, "v", lambda d: t1.at[slab(v, d, 128)], 128, F32, m["bv"])

    def start(stage):
        stage.send_far()
        stage.send_plus()
        stage.send_minus()

    images[2] = image_slab(2)
    far.send_far()
    images[1] = image_slab(1)
    images[-1] = image_slab(-1)
    far.send_plus()
    far.send_minus()
    start(plus)
    images[0] = image_slab(0)
    far.relay()
    start(minus)
    plus.relay()
    start(own)
    far.finish(t1.at[slab(v, 2, 128)])
    down.send_far()
    minus.relay()
    plus.finish(t1.at[slab(v, 1, 128)])
    down.send_plus()
    own.relay()
    minus.finish(t1.at[slab(v, -1, 128)])
    down.send_minus()
    down.relay()
    own.finish(t1.at[slab(v, 0, 128)])
    down.finish(t2)
    copies = []
    for i, d in enumerate((1, -1, 2)):
        copy = links.copy(links.slot(), t2.at[slab(w, d, 32)], from_w.at[i], place.along("w", d))
        copy.start()
        copies.append(copy)
    for copy in copies:
        copy.wait()
    for stage in (far, plus, minus, own, down):
        stage.drain()
    return t2[slab(w, 0, 32), :] + ((from_w[0] + from_w[1]) + from_w[2])


def sub(x, c):
    return jnp.broadcast_to(x[c : c + 1, :], (8, 128))


def lane(x, j):
    return jnp.broadcast_to(x[:, j : j + 1], (8, 128))


HIGH = lax.Precision.HIGHEST
TT = (((1,), (1,)), ((), ()))


def dot6(a, b):
    return lax.dot_general(a, b, TT, precision=HIGH, preferred_element_type=F32)


def split(a):
    high = a.astype(BF16)
    return high, (a - high.astype(F32)).astype(BF16)


def dot3(a, b):
    def one(p, q):
        return lax.dot_general(p, q, TT, preferred_element_type=F32)

    return one(a[0], b[0]) + (one(a[0], b[1]) + one(a[1], b[0]))


def inverse_factor_128(a_rows, w_rows, between):
    row_id = lax.broadcasted_iota(jnp.int32, (8, 128), 0)
    out = []
    for p in range(16):
        j0 = 8 * p
        va, vw = a_rows[p], w_rows[p]
        diag = [lane(va, j0 + b) for b in range(8)]
        tops, inverses, rows = [], [], []
        scale = final = None
        for c in range(8):
            pivot = sub(diag[c], c)
            row = {b: sub(diag[b], c) for b in range(c + 1, 8)}
            product = diag[c] * row[c + 1] if c < 7 else None
            q = 1.0 / pivot
            ua, uw = sub(va, c), sub(vw, c)
            if c < 7:
                diag[c + 1] = diag[c + 1] - product * q
                f = diag[c] * q
                va, vw = va - f * ua, vw - f * uw
                for b in range(c + 2, 8):
                    diag[b] = diag[b] - f * row[b]
            scale = pivot if c == 0 else jnp.where(row_id == c, pivot, scale)
            final = uw if c == 0 else jnp.where(row_id == c, uw, final)
            tops.append((ua, uw))
            inverses.append(q)
            rows.append(row)
        out.append(final * lax.rsqrt(scale))
        for i in range(p + 1, 16):
            below = [lane(a_rows[i], j0 + b) for b in range(8)]
            a, w = a_rows[i], w_rows[i]
            for c in range(8):
                f = below[c] * inverses[c]
                a, w = a - f * tops[c][0], w - f * tops[c][1]
                for b in range(c + 1, 8):
                    below[b] = below[b] - f * rows[c][b]
            a_rows[i], w_rows[i] = a, w
        between(p)
    return out


def factor_apply(s, zs, chunks, out, ad, wp, lp, fill):
    row_id = lax.broadcasted_iota(jnp.int32, (8, 128), 0)
    lane_id = lax.broadcasted_iota(jnp.int32, (8, 128), 1)
    ad[...] = s[0:128, 0:128]
    wp[...] = jnp.zeros((128, 128), F32)
    lp[...] = jnp.zeros((512, 128), F32)

    def step(kb, carry):
        prev = pl.ds(mo(jnp.maximum(kb - 1, 0) * 128, 128), 128)
        col = pl.ds(mo(kb * 128, 128), 128)
        a_rows = [ad[8 * i : 8 * i + 8, :] for i in range(16)]
        w_rows = [jnp.where(lane_id == row_id + 8 * i, 1.0, 0.0) for i in range(16)]
        inverse = split(wp[...])

        def gram_chunk(i):
            r = slice(i * 128, i * 128 + 128)
            s[r, :] = s[r, :] - dot6(lp[r, :], lp[...])

        def row_chunk(lo, n):
            r = slice(lo, lo + n)
            c = dot3(split(zs[r, prev]), inverse)
            out[r, prev] = c
            zs[r, :] = zs[r, :] - dot3(split(c), split(lp[...]))

        work = [functools.partial(gram_chunk, i) for i in range(4)]
        work += [functools.partial(row_chunk, lo, n) for lo, n in chunks]

        def between(p):
            if p % 2 == 1 and work:
                work.pop(0)()
            while p == 15 and work:
                work.pop(0)()

        rows = inverse_factor_128(a_rows, w_rows, between)
        for i in range(16):
            wp[8 * i : 8 * i + 8, :] = rows[i]
        new = dot6(s[:, col], wp[...])
        below = lax.broadcasted_iota(jnp.int32, (512, 128), 0) >= (kb + 1) * 128
        lp[...] = jnp.where(below, new, 0.0)
        following = pl.ds(mo(jnp.minimum(kb + 1, 3) * 128, 128), 128)
        ad[...] = s[following, following] - dot6(lp[following, :], lp[following, :])

        @pl.when(kb == 0)
        def _():
            fill()

        return carry

    lax.fori_loop(0, 4, step, 0)
    inverse = split(wp[...])
    for lo, n in chunks:
        out[lo : lo + n, 384:512] = dot3(split(zs[lo : lo + n, 384:512]), inverse)


def selections():
    s0 = np.zeros((2, 512, 128), np.float32)
    s1 = np.zeros((2, 128, 128), np.float32)
    r = np.arange(32)
    for lo in range(2):
        for y in range(4):
            s0[lo, y * 128 + lo * 64 + r, y * 32 + r] = 1
        for hi in range(2):
            s1[hi, (lo * 2 + 1) * 32 + r, (hi * 2 + lo) * 32 + r] = 1
    return jnp.asarray(s0, BF16), jnp.asarray(s1, BF16)


def bands(n, dtype):
    h = n // 2
    shapes = [(n, K), (n, K), (n, K), (h, K), (h, K), (n, K), (n, K)]
    return [pltpu.VMEM(shape, dtype) for shape in shapes]


PLANE = [(dv, dw) for dv in range(4) for dw in range(4) if dv or dw]
CHUNKS = [(i * 128, 128) for i in range(4)]
SCRATCH = {
    "packed": pltpu.VMEM((2, 256, 2048), BF16),
    "raw": pltpu.VMEM((512, 2048), BF16),
    "xf": pltpu.VMEM((512, 2048), BF16),
    "xt": pltpu.VMEM((2048, 512), BF16),
    "b0": pltpu.VMEM((2048, K), BF16),
    "rows": pltpu.VMEM((256, 4096), BF16),
    "rows_sem": pltpu.SemaphoreType.DMA,
    "ring_sums": pltpu.VMEM((4, 16, 128), F32),
    "plane_sums": pltpu.VMEM((16, 16, 128), F32),
    "pa": pltpu.VMEM((512, K), F32),
    "pb": pltpu.VMEM((512, K), F32),
    "proj": pltpu.VMEM((512, K), BF16),
    "y": pltpu.VMEM((2, 32, 2 * K), BF16),
    "yb": pltpu.VMEM((2048, 2 * K), BF16),
    "img": pltpu.VMEM((4, 512, K), F32),
    "t1": pltpu.VMEM((512, K), F32),
    "t2": pltpu.VMEM((128, K), F32),
    "za": pltpu.VMEM((512, 2 * K), F32),
    "ga": pltpu.VMEM((512, 2 * K), F32),
    "mine": pltpu.VMEM((1024, K), F32),
    "theirs": pltpu.VMEM((2, 1024, K), F32),
    "bu": bands(512, BF16),
    "bv": bands(128, F32),
    "bw": pltpu.VMEM((3, 32, K), F32),
    "s": pltpu.VMEM((512, 512), F32),
    "zs": pltpu.VMEM((544, 512), F32),
    "out": pltpu.VMEM((544, 512), F32),
    "ad": pltpu.VMEM((128, 128), F32),
    "wp": pltpu.VMEM((128, 128), F32),
    "lp": pltpu.VMEM((512, 128), F32),
    "labs": pltpu.VMEM((512, 128), BF16),
    "lb": pltpu.VMEM((4, 2, 16, 256), BF16),
    "units": pltpu.VMEM((512, K), BF16),
    "ub": pltpu.VMEM((4, 2, 256, K), BF16),
    "best": pltpu.VMEM((512, 128), F32),
    "tops": pltpu.VMEM((2, 8, 512), F32),
}


def first_product(links, place, load, sb_ref, s0_ref, s1_ref, ids_ref, m):
    u, v, w, k = (*(place.coord[a] for a in "uvw"), place.k)
    z, xl = place.z, place.x % 2
    partner = place.partner()
    e_ref, packed, raw, xf, xt, b0 = (m[n] for n in ("rows", "packed", "raw", "xf", "xt", "b0"))
    ring_sums, plane_sums = m["ring_sums"], m["plane_sums"]
    gather = flood(links, place, b0, sb_ref)
    next(gather)
    b0[pl.ds(mo((u * 16 + v * 4 + w) * 32, 32), 32), :] = sb_ref[...]

    def pack(t, carry):
        x, q = t // 4, t % 4
        tiles = [e_ref[:, pl.ds(mo((((x // 2) * 4 + y) * 4 + q) * 128, 128), 128)] for y in range(4)]
        lanes = pl.ds(mo(t * 128, 128), 128)
        packed[0, :, lanes] = jnp.dot(
            jnp.concatenate(tiles, axis=1), s0_ref[x % 2], preferred_element_type=F32
        ).astype(BF16)
        near = jnp.dot(e_ref[:, lanes], s1_ref[0], preferred_element_type=F32)
        far = jnp.dot(e_ref[:, pl.ds(mo(2048 + t * 128, 128), 128)], s1_ref[1], preferred_element_type=F32)
        packed[1, :, lanes] = (near + far).astype(BF16)
        return carry

    load.wait()
    lax.fori_loop(0, 16, pack, 0, unroll=True)
    mine = pl.ds(mo(k * 256, 256), 256)
    swap_rows = links.copy(links.slot(), packed.at[1 - k], raw.at[mine], partner)
    swap_rows.start()
    raw[mine, :] = packed[k]
    labs, lb = m["labs"], m["lb"]
    ids = jnp.broadcast_to(ids_ref[...].astype(F32), (128, 256))
    labs[mine, :] = ids.T.astype(BF16)
    lb[z, xl] = ids[0:16, :].astype(BF16)
    small = [links.copy(links.slot(), labs.at[mine], labs.at[mine], partner)]
    for dz in range(4):
        for dx in range(2):
            if dz or dx:
                device = place.at(dx * (1 - 2 * xl), 0, dz, k)
                small.append(links.copy(links.slot(), lb.at[z, xl], lb.at[z, xl], device))
    for copy in small:
        copy.start()
    next(gather)
    swap_rows.wait()

    total = jnp.dot(jnp.ones((8, 512), BF16), raw[...], preferred_element_type=F32)
    for i in range(16):
        ring_sums[u, i : i + 1, :] = total[0:1, i * 128 : i * 128 + 128]
    ring = [
        links.copy(links.slot(), ring_sums.at[u], ring_sums.at[u], place.along("u", d)) for d in (1, -1, 2)
    ]
    for copy in ring:
        copy.start()
    next(gather)
    for copy in ring:
        copy.wait()
    here = v * 4 + w
    plane_sums[here] = (ring_sums[0] + ring_sums[1]) + (ring_sums[2] + ring_sums[3])
    plane = [
        links.copy(links.slot(), plane_sums.at[here], plane_sums.at[here], place.in_plane(dv, dw))
        for dv, dw in PLANE
    ]
    for copy in plane:
        copy.start()
    next(gather)
    next(gather)
    for copy in plane:
        copy.wait()
    average = jnp.sum(plane_sums[...], axis=0) / ROWS
    for i in range(16):
        lanes = slice(i * 128, i * 128 + 128)
        xf[:, lanes] = (raw[:, lanes].astype(F32) - average[i : i + 1, :]).astype(BF16)

    def turn(t, carry):
        lanes = pl.ds(mo(t * 128, 128), 128)
        xt[lanes, :] = xf[:, lanes].T
        return carry

    pa, pb, proj = m["pa"], m["pb"], m["proj"]

    def product(d, first=False):
        slab = pl.ds(mo(((u + d + 4) % 4) * 512, 512), 512)
        term = jnp.dot(xf[:, slab], b0[slab, :], preferred_element_type=F32)
        pa[...] = term if first else pa[...] + term

    product(0, first=True)
    product(1)
    product(-1)
    next(gather)
    product(2)
    swap = links.copy(links.slot(), pa, pb, partner)
    swap.start()
    lax.fori_loop(0, 16, turn, 0)
    next(gather, None)
    for copy in small:
        copy.wait()
    swap.wait()
    proj[...] = (pa[...] + pb[...]).astype(BF16)


def power_step(links, place, step, m):
    xf, xt, proj, yb, img, za, ga = (m[n] for n in ("xf", "xt", "proj", "yb", "img", "za", "ga"))
    mine, theirs, own_y = m["mine"], m["theirs"].at[step], m["y"].at[step]
    u, v, w = (place.coord[a] for a in "uvw")

    def image_slab(d):
        start = mo(((u + d + 4) % 4) * 512, 512)
        img[d % 4] = jnp.dot(xt[pl.ds(start, 512), :], proj[...], preferred_element_type=F32)
        return img.at[d % 4]

    image = reduce_image(links, place, image_slab, m) * (1.0 / ROWS)
    high = image.astype(BF16)
    own_y[:, 0:K] = high
    own_y[:, K : 2 * K] = (image - high.astype(F32)).astype(BF16)
    yb[pl.ds(mo((u * 16 + v * 4 + w) * 32, 32), 32), :] = own_y[...]

    def slab(d):
        return pl.ds(mo(((u + d + 4) % 4) * 512, 512), 512)

    def gram(d, first=False):
        term = lax.dot_general(
            yb[slab(d), 0:K], yb[slab(d), :], (((0,), (0,)), ((), ())), preferred_element_type=F32
        )
        ga[...] = term if first else ga[...] + term

    def product(d, first=False):
        term = jnp.dot(xf[:, slab(d)], yb[slab(d), :], preferred_element_type=F32)
        za[...] = term if first else za[...] + term

    gather = flood(links, place, yb, own_y)
    for ready in gather:
        if ready == (2,):
            break
        for d in ready or ():
            gram(d, d == 0)
            product(d, d == 0)
    partner = place.partner()
    top, bottom = pl.ds(0, 512), pl.ds(512, 512)
    gram(2)
    cross = ga[:, K : 2 * K]
    mine[bottom, :] = ga[:, 0:K] + (cross + cross.T)
    swap_gram = links.copy(links.slot(), mine.at[bottom], theirs.at[bottom], partner)
    swap_gram.start()
    product(2)
    mine[top, :] = za[:, 0:K] + za[:, K : 2 * K]
    swap_rows = links.copy(links.slot(), mine.at[top], theirs.at[top], partner)
    swap_rows.start()
    next(gather, None)
    swap_gram.wait()
    m["s"][...] = mine[bottom, :] + theirs[bottom, :]

    def fill():
        swap_rows.wait()
        m["zs"][0:512, :] = mine[top, :] + theirs[top, :]

    return fill


class UpDown:
    def __init__(self, links, place, ub, x, lo):
        self.links, self.ub, self.x, self.lo, self.z = links, ub, x, lo, place.z
        self.up, self.down = place.at(0, 0, 1, place.k), place.at(0, 0, -1, place.k)
        self.slots = [links.slot() for _ in range(4)]
        self.sent = []

    def part(self, d, lo=0, n=128):
        return self.ub.at[(self.z + d + 4) % 4, self.x, pl.ds(self.lo + lo, n)]

    def _send(self, i, ref, device):
        copy = self.links.copy(self.slots[i], ref, ref, device)
        copy.start()
        self.sent.append(copy)

    def start(self):
        self._send(0, self.part(0), self.up)
        self._send(1, self.part(0), self.down)

    def relay(self):
        self.links.arrived(self.slots[0], self.part(-1), self.up)
        self._send(2, self.part(-1, 0, 64), self.up)
        self.links.arrived(self.slots[1], self.part(1), self.up)
        self._send(3, self.part(1, 64, 64), self.down)

    def far(self):
        self.links.arrived(self.slots[2], self.part(2, 0, 64), self.up)
        self.links.arrived(self.slots[3], self.part(2, 64, 64), self.up)


def nearest_rows(links, place, limit, out, m):
    z, k, xl = place.z, place.k, place.x % 2
    units, ub, lb, labs, best, tops = (m[n] for n in ("units", "ub", "lb", "labs", "best", "tops"))
    across = place.at(1 - 2 * xl, 0, 0, k)
    ub[z, xl] = units[pl.ds(mo(k * 256, 256), 256), :]
    sent = []
    slots = [links.slot() for _ in range(5)]

    def cross(i, d, lo):
        ref = ub.at[(z + d + 4) % 4, xl, pl.ds(lo, 128)]
        copy = links.copy(slots[i], ref, ref, across)
        copy.start()
        sent.append(copy)

    def crossed(i, d, lo):
        links.arrived(slots[i], ub.at[(z + d + 4) % 4, 1 - xl, pl.ds(lo, 128)], across)

    ga = UpDown(links, place, ub, xl, 0)
    gb = UpDown(links, place, ub, xl, 128)
    gc = UpDown(links, place, ub, 1 - xl, 0)
    cross(0, 0, 0)
    gb.start()
    ga.start()
    cross(1, 0, 128)
    best[...] = jnp.full((512, 128), -1.0, F32)
    bound = limit[0]
    lane_id = lax.broadcasted_iota(jnp.int32, (1, 128), 1)
    own_first = (z * 4 + xl * 2) * 256

    def score(d, x):
        zz = (z + d + 4) % 4
        labels = lb[zz, x][0:1, :].astype(F32)
        first = (zz * 4 + x * 2 + k) * 256

        def part(r, n):
            value = lax.dot_general(units[pl.ds(r, n), :], ub[zz, x], TT, preferred_element_type=F32)
            rows = lax.broadcasted_iota(jnp.int32, (n, 128), 0) + (own_first + r)
            label = labs[pl.ds(r, n), :].astype(F32)
            top = best[pl.ds(r, n), :]
            for t in range(2):
                lanes = slice(t * 128, t * 128 + 128)
                other = lane_id + (first + t * 128)
                use = (label == labels[:, lanes]) & (other < bound) & (other != rows)
                top = jnp.maximum(top, jnp.where(use, value[:, lanes], -1.0))
            best[pl.ds(r, n), :] = top

        rows_loop(512, 256, part)

    score(0, xl)
    crossed(0, 0, 0)
    gc.start()
    gb.relay()
    cross(2, -1, 128)
    cross(3, 1, 128)
    ga.relay()
    gb.far()
    cross(4, 2, 128)

    def pair(i, carry):
        score(2 * i - 1, xl)
        return carry

    lax.fori_loop(0, 2, pair, 0)
    gc.relay()
    crossed(1, 0, 128)
    score(0, 1 - xl)
    ga.far()
    score(2, xl)
    crossed(2, -1, 128)
    crossed(3, 1, 128)

    def other_pair(i, carry):
        score(2 * i - 1, 1 - xl)
        return carry

    lax.fori_loop(0, 2, other_pair, 0)
    gc.far()
    crossed(4, 2, 128)
    score(2, 1 - xl)
    for copy in sent + ga.sent + gb.sent + gc.sent:
        copy.wait_send()
    top = jnp.max(best[...].T, axis=0, keepdims=True)
    tops[0] = jnp.broadcast_to(top, (8, 512))
    swap = links.copy(links.slot(), tops.at[0], tops.at[1], place.partner())
    swap.start()
    swap.wait()
    top = jnp.maximum(tops[0], tops[1])[0:1, :]
    out[...] = jnp.where(k == 0, top[:, 0:256], top[:, 256:512])


def whole_kernel(
    e_ref, sb_ref, s0_ref, s1_ref, ids_ref, limit, subspace, nearest, send, recv, m
):
    links, place = Links(send, recv), Place()
    k, xl = place.k, place.x % 2
    load = pltpu.make_async_copy(e_ref, m["rows"], m["rows_sem"])
    load.start()
    devices = [place.along("u", d) for d in (1, -1, 2)] + [place.partner()]
    devices += [place.in_plane(dv, dw) for dv, dw in PLANE]
    flip = 1 - 2 * xl
    devices += [place.at(flip, 0, dz, k) for dz in (1, 2, 3)]
    greet(devices)
    first_product(links, place, load, sb_ref, s0_ref, s1_ref, ids_ref, m)
    s, zs, out, ad, wp, lp = (m[n] for n in ("s", "zs", "out", "ad", "wp", "lp"))
    fill = power_step(links, place, 0, m)
    factor_apply(s, zs, CHUNKS, out, ad, wp, lp, fill)
    m["proj"][...] = out[0:512, :].astype(BF16)
    fill = power_step(links, place, 1, m)
    own_y = m["y"].at[1]
    zs[512:544, :] = own_y[:, 0:K].astype(F32) + own_y[:, K : 2 * K].astype(F32)
    factor_apply(s, zs, CHUNKS + [(512, 32)], out, ad, wp, lp, fill)
    units = m["units"]
    for i in range(4):
        coords = out[i * 128 : i * 128 + 128, :]
        size = jnp.sum(coords * coords, axis=1, keepdims=True) + EPS
        units[i * 128 : i * 128 + 128, :] = (coords * lax.rsqrt(size)).astype(BF16)
    subspace[...] = out[512:544, :] * math.sqrt(D)
    nearest_rows(links, place, limit, nearest, m)
    assert links.used <= SLOTS


def body(embeddings, start_basis, cluster_ids, valid_counts):
    s0, s1 = selections()
    vmem = pl.BlockSpec(memory_space=pltpu.VMEM)
    subspace, nearest = pl.pallas_call(
        whole_kernel,
        out_shape=[jax.ShapeDtypeStruct((32, K), F32), jax.ShapeDtypeStruct((1, 256), F32)],
        in_specs=[pl.BlockSpec(memory_space=pl.ANY)] + [vmem] * 4 + [pl.BlockSpec(memory_space=pltpu.SMEM)],
        out_specs=[vmem] * 2,
        scratch_shapes=[pltpu.SemaphoreType.DMA((SLOTS,)), pltpu.SemaphoreType.DMA((SLOTS,)), SCRATCH],
        compiler_params=pltpu.CompilerParams(
            collective_id=0, has_side_effects=True, vmem_limit_bytes=VMEM_LIMIT
        ),
        name="whole",
    )(embeddings, start_basis, s0, s1, cluster_ids.reshape(1, 256), valid_counts)
    return (subspace, nearest.reshape(256))


def solution(mesh):
    placed = (
        P(("cluster", "member"), None),
        P(("cluster", "member"), None),
        P(("cluster", "member")),
        P("cluster"),
    )
    return jax.shard_map(
        body,
        mesh=mesh,
        in_specs=placed,
        out_specs=(P(("cluster", "member"), None), P(("cluster", "member"))),
        check_vma=False,
    )
```

```python
import functools
import math

import jax
import jax.numpy as jnp
import numpy as np
from jax import lax
from jax.experimental import pallas as pl
from jax.experimental.pallas import tpu as pltpu
from jax.sharding import PartitionSpec as P

EPS = 1e-06
MESH = pl.DeviceIdType.MESH
F32 = jnp.float32
BF16 = jnp.bfloat16
D = 4096
K = 512
ROWS = 32768
VMEM_LIMIT = 60 * 1024 * 1024
SLOTS = 384


class Links:
    def __init__(self, send, recv):
        self.send, self.recv, self.used = send, recv, 0

    def slot(self):
        self.used += 1
        return self.used - 1

    def copy(self, slot, src, dst, device):
        return pltpu.make_async_remote_copy(
            src_ref=src,
            dst_ref=dst,
            send_sem=self.send.at[slot],
            recv_sem=self.recv.at[slot],
            device_id=device,
            device_id_type=MESH,
        )

    def arrived(self, slot, dst, device):
        self.copy(slot, dst, dst, device).wait_recv()


class Place:
    def __init__(self):
        c, m = lax.axis_index("cluster"), lax.axis_index("member")
        self.x = (c // 4) * 2 + (m // 2) % 2
        self.y = c % 4
        self.z = m // 4
        self.k = m % 2
        k, o = self.k, 1 - self.k
        self.coord = {
            "u": self.x * o + self.y * k,
            "v": self.z,
            "w": self.y * o + self.x * k,
        }

    def at(self, dx, dy, dz, core):
        x = (self.x + dx + 4) % 4
        y = (self.y + dy + 4) % 4
        z = (self.z + dz + 4) % 4
        return ((x // 2) * 4 + y, z * 4 + (x % 2) * 2 + core)

    def along(self, axis, d):
        k, o = self.k, 1 - self.k
        if axis == "u":
            return self.at(d * o, d * k, 0, k)
        if axis == "v":
            return self.at(0, 0, d, k)
        return self.at(d * k, d * o, 0, k)

    def in_plane(self, dv, dw):
        return self.at(dw * self.k, dw * (1 - self.k), dv, self.k)

    def partner(self):
        return self.at(0, 0, 0, 1 - self.k)


def greet(devices):
    barrier = pltpu.get_barrier_semaphore()
    for device in devices:
        pl.semaphore_signal(barrier, inc=1, device_id=device, device_id_type=MESH)
    pl.semaphore_wait(barrier, len(devices))


def mo(i, n):
    return pl.multiple_of(i, n)


class GatherStage:
    def __init__(self, links, place, axis, buf, base, n, stride, source=None):
        self.links, self.buf, self.n, self.h = links, buf, n, n // 2
        self.base, self.stride, self.coord = base, stride, place.coord[axis]
        self.plus, self.minus = place.along(axis, 1), place.along(axis, -1)
        self.slots = [links.slot() for _ in range(4)]
        self.source = source
        self.sent = []

    def region(self, d, part=None):
        start = mo(self.base + ((self.coord + d + 4) % 4) * self.stride, self.n)
        if part is None:
            return self.buf.at[pl.ds(start, self.n)]
        return self.buf.at[pl.ds(mo(start + part * self.h, self.h), self.h)]

    def _send(self, i, src, dst, device):
        copy = self.links.copy(self.slots[i], src, dst, device)
        copy.start()
        self.sent.append(copy)

    def start(self):
        own = self.region(0)
        src = own if self.source is None else self.source
        self._send(0, src, own, self.plus)
        self._send(1, src, own, self.minus)

    def relay(self):
        self.links.arrived(self.slots[0], self.region(-1), self.plus)
        first = self.region(-1, 0)
        self._send(2, first, first, self.plus)
        self.links.arrived(self.slots[1], self.region(1), self.plus)
        second = self.region(1, 1)
        self._send(3, second, second, self.minus)

    def far(self):
        self.links.arrived(self.slots[2], self.region(2, 0), self.plus)
        self.links.arrived(self.slots[3], self.region(2, 1), self.plus)

    def drain(self):
        for copy in self.sent:
            copy.wait_send()


class DirectStage(GatherStage):
    def __init__(self, links, place, axis, *rest, **more):
        super().__init__(links, place, axis, *rest, **more)
        self.opposite = place.along(axis, 2)

    def start(self):
        super().start()
        own = self.region(0)
        src = own if self.source is None else self.source
        self._send(2, src, own, self.opposite)

    def near(self):
        self.links.arrived(self.slots[0], self.region(-1), self.plus)
        self.links.arrived(self.slots[1], self.region(1), self.plus)

    def far(self):
        self.links.arrived(self.slots[2], self.region(2), self.plus)


def flood(links, place, buf, source):
    u, v, w = (place.coord[a] for a in "uvw")

    def ahead(c, d):
        return (c + d + 4) % 4

    own = {0: source}
    wst = DirectStage(links, place, "w", buf, (u * 16 + v * 4) * 32, 32, 32, source=source)
    vst = {
        e: GatherStage(links, place, "v", buf, u * 512 + ahead(w, e) * 32, 32, 128, source=own.get(e))
        for e in (0, -1, 1, 2)
    }
    ust = {
        (f, e): GatherStage(
            links, place, "u", buf, ahead(v, f) * 128 + ahead(w, e) * 32, 32, 512, source=source if f == e == 0 else None
        )
        for f in (0, -1, 1, 2)
        for e in (0, -1, 1, 2)
    }
    wst.start()
    vst[0].start()
    ust[0, 0].start()
    yield None
    wst.near()
    for e in (-1, 1):
        vst[e].start()
        ust[0, e].start()
    vst[0].relay()
    for f in (-1, 1):
        ust[f, 0].start()
    ust[0, 0].relay()
    yield None
    wst.far()
    vst[2].start()
    ust[0, 2].start()
    for e in (-1, 1):
        vst[e].relay()
        for f in (-1, 1):
            ust[f, e].start()
    for e in (-1, 1):
        ust[0, e].relay()
    vst[0].far()
    ust[2, 0].start()
    yield None
    vst[2].relay()
    for f in (-1, 1):
        ust[f, 2].start()
        ust[f, 0].relay()
    ust[0, 2].relay()
    for e in (-1, 1, 2):
        vst[e].far()
        ust[2, e].start()
    yield (0,)
    late = [(f, e) for e in (-1, 1) for f in (-1, 1)] + [(2, 0), (-1, 2), (1, 2), (2, -1), (2, 1), (2, 2)]
    for piece in late:
        ust[piece].relay()
    yield (1, -1)
    for stage in ust.values():
        stage.far()
    yield (2,)
    for stage in [wst, *vst.values(), *ust.values()]:
        stage.drain()


def rows_loop(total, step, fn):
    if total <= step:
        fn(0, total)
        return

    def body(i, carry):
        fn(mo(i * step, step), step)
        return carry

    lax.fori_loop(0, total // step, body, 0)


class ScatterStage:
    def __init__(self, links, place, axis, term, n, dtype, bufs):
        self.links, self.term, self.h, self.dtype = links, term, n // 2, dtype
        self.s2, self.sp, self.sm, self.ra, self.rb, self.rp, self.rm = bufs
        self.plus, self.minus = place.along(axis, 1), place.along(axis, -1)
        self.slots = [links.slot() for _ in range(6)]
        self.low, self.high = pl.ds(0, n // 2), pl.ds(n // 2, n // 2)
        self.sent = []

    def _send(self, i, src, dst, device):
        copy = self.links.copy(self.slots[i], src, dst, device)
        copy.start()
        self.sent.append(copy)

    def _got(self, i, dst):
        self.links.arrived(self.slots[i], dst, self.plus)

    def send_far(self):
        self.s2[...] = self.term(2)[...].astype(self.dtype)
        self._send(0, self.s2.at[self.low], self.ra, self.plus)
        self._send(1, self.s2.at[self.high], self.rb, self.minus)

    def send_plus(self):
        self.sp[self.high, :] = self.term(1)[self.high, :].astype(self.dtype)
        self._send(2, self.sp.at[self.high], self.rp.at[self.high], self.plus)

    def send_minus(self):
        self.sm[self.low, :] = self.term(-1)[self.low, :].astype(self.dtype)
        self._send(3, self.sm.at[self.low], self.rm.at[self.low], self.minus)

    def relay(self):
        self._got(0, self.ra)
        self.sp[self.low, :] = (self.term(1)[self.low, :] + self.ra[...].astype(F32)).astype(self.dtype)
        self._send(4, self.sp.at[self.low], self.rp.at[self.low], self.plus)
        self._got(1, self.rb)
        self.sm[self.high, :] = (self.term(-1)[self.high, :] + self.rb[...].astype(F32)).astype(self.dtype)
        self._send(5, self.sm.at[self.high], self.rm.at[self.high], self.minus)

    def finish(self, out):
        self._got(2, self.rp.at[self.high])
        self._got(3, self.rm.at[self.low])
        self._got(4, self.rp.at[self.low])
        self._got(5, self.rm.at[self.high])
        out[...] = self.term(0)[...] + (self.rp[...].astype(F32) + self.rm[...].astype(F32))

    def drain(self):
        for copy in self.sent:
            copy.wait_send()


def reduce_image(links, place, image_slab, m):
    u, v, w = (place.coord[a] for a in "uvw")
    t1, t2, from_w = m["t1"], m["t2"], m["bw"]

    def slab(c, d, n):
        return pl.ds(mo(((c + d + 4) % 4) * n, n), n)

    images = {}

    def piece(i, f):
        rows = slab(v, f, 128)
        full, half = pl.ds(i * 128, 128), pl.ds(i * 64, 64)
        bufs = [ref.at[half if j in (3, 4) else full] for j, ref in enumerate(m["bu"])]
        return ScatterStage(links, place, "u", lambda d: images[d].at[rows], 128, BF16, bufs)

    far, plus, minus, own = (piece(i, f) for i, f in enumerate((2, 1, -1, 0)))
    down = ScatterStage(links, place, "v", lambda d: t1.at[slab(v, d, 128)], 128, F32, m["bv"])

    def start(stage):
        stage.send_far()
        stage.send_plus()
        stage.send_minus()

    images[2] = image_slab(2)
    far.send_far()
    images[1] = image_slab(1)
    images[-1] = image_slab(-1)
    far.send_plus()
    far.send_minus()
    start(plus)
    images[0] = image_slab(0)
    far.relay()
    start(minus)
    plus.relay()
    start(own)
    far.finish(t1.at[slab(v, 2, 128)])
    down.send_far()
    minus.relay()
    plus.finish(t1.at[slab(v, 1, 128)])
    down.send_plus()
    own.relay()
    minus.finish(t1.at[slab(v, -1, 128)])
    down.send_minus()
    down.relay()
    own.finish(t1.at[slab(v, 0, 128)])
    down.finish(t2)
    copies = []
    for i, d in enumerate((1, -1, 2)):
        copy = links.copy(links.slot(), t2.at[slab(w, d, 32)], from_w.at[i], place.along("w", d))
        copy.start()
        copies.append(copy)
    for copy in copies:
        copy.wait()
    for stage in (far, plus, minus, own, down):
        stage.drain()
    return t2[slab(w, 0, 32), :] + ((from_w[0] + from_w[1]) + from_w[2])


def sub(x, c):
    return jnp.broadcast_to(x[c : c + 1, :], (8, 128))


def lane(x, j):
    return jnp.broadcast_to(x[:, j : j + 1], (8, 128))


HIGH = lax.Precision.HIGHEST
TT = (((1,), (1,)), ((), ()))


def dot6(a, b):
    return lax.dot_general(a, b, TT, precision=HIGH, preferred_element_type=F32)


def split(a):
    high = a.astype(BF16)
    return high, (a - high.astype(F32)).astype(BF16)


def dot3(a, b):
    def one(p, q):
        return lax.dot_general(p, q, TT, preferred_element_type=F32)

    return one(a[0], b[0]) + (one(a[0], b[1]) + one(a[1], b[0]))


def inverse_factor_128(a_rows, w_rows, between):
    row_id = lax.broadcasted_iota(jnp.int32, (8, 128), 0)
    out = []
    for p in range(16):
        j0 = 8 * p
        va, vw = a_rows[p], w_rows[p]
        diag = [lane(va, j0 + b) for b in range(8)]
        tops, inverses, rows = [], [], []
        scale = final = None
        for c in range(8):
            pivot = sub(diag[c], c)
            row = {b: sub(diag[b], c) for b in range(c + 1, 8)}
            product = diag[c] * row[c + 1] if c < 7 else None
            q = 1.0 / pivot
            ua, uw = sub(va, c), sub(vw, c)
            if c < 7:
                diag[c + 1] = diag[c + 1] - product * q
                f = diag[c] * q
                va, vw = va - f * ua, vw - f * uw
                for b in range(c + 2, 8):
                    diag[b] = diag[b] - f * row[b]
            scale = pivot if c == 0 else jnp.where(row_id == c, pivot, scale)
            final = uw if c == 0 else jnp.where(row_id == c, uw, final)
            tops.append((ua, uw))
            inverses.append(q)
            rows.append(row)
        out.append(final * lax.rsqrt(scale))
        for i in range(p + 1, 16):
            below = [lane(a_rows[i], j0 + b) for b in range(8)]
            a, w = a_rows[i], w_rows[i]
            for c in range(8):
                f = below[c] * inverses[c]
                a, w = a - f * tops[c][0], w - f * tops[c][1]
                for b in range(c + 1, 8):
                    below[b] = below[b] - f * rows[c][b]
            a_rows[i], w_rows[i] = a, w
        between(p)
    return out


def factor_apply(s, zs, chunks, out, ad, wp, lp, fill):
    row_id = lax.broadcasted_iota(jnp.int32, (8, 128), 0)
    lane_id = lax.broadcasted_iota(jnp.int32, (8, 128), 1)
    ad[...] = s[0:128, 0:128]
    wp[...] = jnp.zeros((128, 128), F32)

    def step(kb, carry):
        prev = pl.ds(mo(jnp.maximum(kb - 1, 0) * 128, 128), 128)
        col = pl.ds(mo(kb * 128, 128), 128)
        a_rows = [ad[8 * i : 8 * i + 8, :] for i in range(16)]
        w_rows = [jnp.where(lane_id == row_id + 8 * i, 1.0, 0.0) for i in range(16)]
        inverse = split(wp[...])

        def column():
            below = lax.broadcasted_iota(jnp.int32, (512, 128), 0) >= kb * 128
            lp[...] = jnp.where(below, dot6(s[:, prev], wp[...]), 0.0)

        def gram_chunk(i):
            r = slice(i * 128, i * 128 + 128)
            s[r, :] = s[r, :] - dot6(lp[r, :], lp[...])

        def row_chunk(lo, n):
            r = slice(lo, lo + n)
            c = dot3(split(zs[r, prev]), inverse)
            out[r, prev] = c
            zs[r, :] = zs[r, :] - dot3(split(c), split(lp[...]))

        column()
        work = [functools.partial(gram_chunk, i) for i in range(4)]
        work += [functools.partial(row_chunk, lo, n) for lo, n in chunks]

        def between(p):
            if p % 2 == 1 and work:
                work.pop(0)()
            while p == 15 and work:
                work.pop(0)()

        rows = inverse_factor_128(a_rows, w_rows, between)
        for i in range(16):
            wp[8 * i : 8 * i + 8, :] = rows[i]
        following = pl.ds(mo(jnp.minimum(kb + 1, 3) * 128, 128), 128)
        corner = dot6(s[following, col], wp[...])
        ad[...] = s[following, following] - dot6(corner, corner)

        @pl.when(kb == 0)
        def _():
            fill()

        return carry

    lax.fori_loop(0, 4, step, 0)
    inverse = split(wp[...])
    for lo, n in chunks:
        out[lo : lo + n, 384:512] = dot3(split(zs[lo : lo + n, 384:512]), inverse)


def selections():
    s0 = np.zeros((2, 512, 128), np.float32)
    s1 = np.zeros((2, 128, 128), np.float32)
    r = np.arange(32)
    for lo in range(2):
        for y in range(4):
            s0[lo, y * 128 + lo * 64 + r, y * 32 + r] = 1
        for hi in range(2):
            s1[hi, (lo * 2 + 1) * 32 + r, (hi * 2 + lo) * 32 + r] = 1
    return jnp.asarray(s0, BF16), jnp.asarray(s1, BF16)


def bands(n, dtype):
    h = n // 2
    shapes = [(n, K), (n, K), (n, K), (h, K), (h, K), (n, K), (n, K)]
    return [pltpu.VMEM(shape, dtype) for shape in shapes]


PLANE = [(dv, dw) for dv in range(4) for dw in range(4) if dv or dw]
CHUNKS = [(i * 128, 128) for i in range(4)]
SCRATCH = {
    "packed": pltpu.VMEM((2, 256, 2048), BF16),
    "raw": pltpu.VMEM((512, 2048), BF16),
    "xf": pltpu.VMEM((512, 2048), BF16),
    "xt": pltpu.VMEM((2048, 512), BF16),
    "b0": pltpu.VMEM((2048, K), BF16),
    "rows": pltpu.VMEM((256, 4096), BF16),
    "rows_sem": pltpu.SemaphoreType.DMA,
    "ring_sums": pltpu.VMEM((4, 16, 128), F32),
    "plane_sums": pltpu.VMEM((16, 16, 128), F32),
    "pa": pltpu.VMEM((512, K), F32),
    "pb": pltpu.VMEM((512, K), F32),
    "proj": pltpu.VMEM((512, K), BF16),
    "y": pltpu.VMEM((2, 32, 2 * K), BF16),
    "yb": pltpu.VMEM((2048, 2 * K), BF16),
    "img": pltpu.VMEM((4, 512, K), F32),
    "t1": pltpu.VMEM((512, K), F32),
    "t2": pltpu.VMEM((128, K), F32),
    "za": pltpu.VMEM((512, 2 * K), F32),
    "ga": pltpu.VMEM((512, 2 * K), F32),
    "mine": pltpu.VMEM((1024, K), F32),
    "theirs": pltpu.VMEM((2, 1024, K), F32),
    "bu": bands(512, BF16),
    "bv": bands(128, F32),
    "bw": pltpu.VMEM((3, 32, K), F32),
    "s": pltpu.VMEM((512, 512), F32),
    "zs": pltpu.VMEM((544, 512), F32),
    "out": pltpu.VMEM((544, 512), F32),
    "ad": pltpu.VMEM((128, 128), F32),
    "wp": pltpu.VMEM((128, 128), F32),
    "lp": pltpu.VMEM((512, 128), F32),
    "labs": pltpu.VMEM((512, 128), BF16),
    "lb": pltpu.VMEM((4, 2, 16, 256), BF16),
    "units": pltpu.VMEM((512, K), BF16),
    "ub": pltpu.VMEM((4, 2, 256, K), BF16),
    "best": pltpu.VMEM((512, 128), F32),
    "tops": pltpu.VMEM((2, 8, 512), F32),
}


def first_product(links, place, load, sb_ref, s0_ref, s1_ref, ids_ref, m):
    u, v, w, k = (*(place.coord[a] for a in "uvw"), place.k)
    z, xl = place.z, place.x % 2
    partner = place.partner()
    e_ref, packed, raw, xf, xt, b0 = (m[n] for n in ("rows", "packed", "raw", "xf", "xt", "b0"))
    ring_sums, plane_sums = m["ring_sums"], m["plane_sums"]
    gather = flood(links, place, b0, sb_ref)
    next(gather)
    b0[pl.ds(mo((u * 16 + v * 4 + w) * 32, 32), 32), :] = sb_ref[...]

    def pack(t, carry):
        x, q = t // 4, t % 4
        tiles = [e_ref[:, pl.ds(mo((((x // 2) * 4 + y) * 4 + q) * 128, 128), 128)] for y in range(4)]
        lanes = pl.ds(mo(t * 128, 128), 128)
        packed[0, :, lanes] = jnp.dot(
            jnp.concatenate(tiles, axis=1), s0_ref[x % 2], preferred_element_type=F32
        ).astype(BF16)
        near = jnp.dot(e_ref[:, lanes], s1_ref[0], preferred_element_type=F32)
        far = jnp.dot(e_ref[:, pl.ds(mo(2048 + t * 128, 128), 128)], s1_ref[1], preferred_element_type=F32)
        packed[1, :, lanes] = (near + far).astype(BF16)
        return carry

    load.wait()
    lax.fori_loop(0, 16, pack, 0, unroll=True)
    mine = pl.ds(mo(k * 256, 256), 256)
    swap_rows = links.copy(links.slot(), packed.at[1 - k], raw.at[mine], partner)
    swap_rows.start()
    raw[mine, :] = packed[k]
    labs, lb = m["labs"], m["lb"]
    ids = jnp.broadcast_to(ids_ref[...].astype(F32), (128, 256))
    labs[mine, :] = ids.T.astype(BF16)
    lb[z, xl] = ids[0:16, :].astype(BF16)
    small = [links.copy(links.slot(), labs.at[mine], labs.at[mine], partner)]
    for dz in range(4):
        for dx in range(2):
            if dz or dx:
                device = place.at(dx * (1 - 2 * xl), 0, dz, k)
                small.append(links.copy(links.slot(), lb.at[z, xl], lb.at[z, xl], device))
    for copy in small:
        copy.start()
    next(gather)
    swap_rows.wait()

    total = jnp.dot(jnp.ones((8, 512), BF16), raw[...], preferred_element_type=F32)
    for i in range(16):
        ring_sums[u, i : i + 1, :] = total[0:1, i * 128 : i * 128 + 128]
    ring = [
        links.copy(links.slot(), ring_sums.at[u], ring_sums.at[u], place.along("u", d)) for d in (1, -1, 2)
    ]
    for copy in ring:
        copy.start()
    next(gather)
    for copy in ring:
        copy.wait()
    here = v * 4 + w
    plane_sums[here] = (ring_sums[0] + ring_sums[1]) + (ring_sums[2] + ring_sums[3])
    plane = [
        links.copy(links.slot(), plane_sums.at[here], plane_sums.at[here], place.in_plane(dv, dw))
        for dv, dw in PLANE
    ]
    for copy in plane:
        copy.start()
    next(gather)
    next(gather)
    for copy in plane:
        copy.wait()
    average = jnp.sum(plane_sums[...], axis=0) / ROWS
    for i in range(16):
        lanes = slice(i * 128, i * 128 + 128)
        xf[:, lanes] = (raw[:, lanes].astype(F32) - average[i : i + 1, :]).astype(BF16)

    def turn(t, carry):
        lanes = pl.ds(mo(t * 128, 128), 128)
        xt[lanes, :] = xf[:, lanes].T
        return carry

    pa, pb, proj = m["pa"], m["pb"], m["proj"]

    def product(d, first=False):
        slab = pl.ds(mo(((u + d + 4) % 4) * 512, 512), 512)
        term = jnp.dot(xf[:, slab], b0[slab, :], preferred_element_type=F32)
        pa[...] = term if first else pa[...] + term

    product(0, first=True)
    product(1)
    product(-1)
    next(gather)
    product(2)
    swap = links.copy(links.slot(), pa, pb, partner)
    swap.start()
    lax.fori_loop(0, 16, turn, 0)
    next(gather, None)
    for copy in small:
        copy.wait()
    swap.wait()
    proj[...] = (pa[...] + pb[...]).astype(BF16)


def power_step(links, place, step, m):
    xf, xt, proj, yb, img, za, ga = (m[n] for n in ("xf", "xt", "proj", "yb", "img", "za", "ga"))
    mine, theirs, own_y = m["mine"], m["theirs"].at[step], m["y"].at[step]
    u, v, w = (place.coord[a] for a in "uvw")

    def image_slab(d):
        start = mo(((u + d + 4) % 4) * 512, 512)
        img[d % 4] = jnp.dot(xt[pl.ds(start, 512), :], proj[...], preferred_element_type=F32)
        return img.at[d % 4]

    image = reduce_image(links, place, image_slab, m) * (1.0 / ROWS)
    high = image.astype(BF16)
    own_y[:, 0:K] = high
    own_y[:, K : 2 * K] = (image - high.astype(F32)).astype(BF16)
    yb[pl.ds(mo((u * 16 + v * 4 + w) * 32, 32), 32), :] = own_y[...]

    def slab(d):
        return pl.ds(mo(((u + d + 4) % 4) * 512, 512), 512)

    def gram(d, first=False):
        term = lax.dot_general(
            yb[slab(d), 0:K], yb[slab(d), :], (((0,), (0,)), ((), ())), preferred_element_type=F32
        )
        ga[...] = term if first else ga[...] + term

    def product(d, first=False):
        term = jnp.dot(xf[:, slab(d)], yb[slab(d), :], preferred_element_type=F32)
        za[...] = term if first else za[...] + term

    gather = flood(links, place, yb, own_y)
    for ready in gather:
        if ready == (2,):
            break
        for d in ready or ():
            gram(d, d == 0)
            product(d, d == 0)
    partner = place.partner()
    top, bottom = pl.ds(0, 512), pl.ds(512, 512)
    gram(2)
    cross = ga[:, K : 2 * K]
    mine[bottom, :] = ga[:, 0:K] + (cross + cross.T)
    swap_gram = links.copy(links.slot(), mine.at[bottom], theirs.at[bottom], partner)
    swap_gram.start()
    product(2)
    mine[top, :] = za[:, 0:K] + za[:, K : 2 * K]
    swap_rows = links.copy(links.slot(), mine.at[top], theirs.at[top], partner)
    swap_rows.start()
    next(gather, None)
    swap_gram.wait()
    m["s"][...] = mine[bottom, :] + theirs[bottom, :]

    def fill():
        swap_rows.wait()
        m["zs"][0:512, :] = mine[top, :] + theirs[top, :]

    return fill


class UpDown:
    def __init__(self, links, place, ub, x, lo):
        self.links, self.ub, self.x, self.lo, self.z = links, ub, x, lo, place.z
        self.up, self.down = place.at(0, 0, 1, place.k), place.at(0, 0, -1, place.k)
        self.slots = [links.slot() for _ in range(4)]
        self.sent = []

    def part(self, d, lo=0, n=128):
        return self.ub.at[(self.z + d + 4) % 4, self.x, pl.ds(self.lo + lo, n)]

    def _send(self, i, ref, device):
        copy = self.links.copy(self.slots[i], ref, ref, device)
        copy.start()
        self.sent.append(copy)

    def start(self):
        self._send(0, self.part(0), self.up)
        self._send(1, self.part(0), self.down)

    def relay(self):
        self.links.arrived(self.slots[0], self.part(-1), self.up)
        self._send(2, self.part(-1, 0, 64), self.up)
        self.links.arrived(self.slots[1], self.part(1), self.up)
        self._send(3, self.part(1, 64, 64), self.down)

    def far(self):
        self.links.arrived(self.slots[2], self.part(2, 0, 64), self.up)
        self.links.arrived(self.slots[3], self.part(2, 64, 64), self.up)


def nearest_rows(links, place, limit, out, m):
    z, k, xl = place.z, place.k, place.x % 2
    units, ub, lb, labs, best, tops = (m[n] for n in ("units", "ub", "lb", "labs", "best", "tops"))
    across = place.at(1 - 2 * xl, 0, 0, k)
    ub[z, xl] = units[pl.ds(mo(k * 256, 256), 256), :]
    sent = []
    slots = [links.slot() for _ in range(5)]

    def cross(i, d, lo):
        ref = ub.at[(z + d + 4) % 4, xl, pl.ds(lo, 128)]
        copy = links.copy(slots[i], ref, ref, across)
        copy.start()
        sent.append(copy)

    def crossed(i, d, lo):
        links.arrived(slots[i], ub.at[(z + d + 4) % 4, 1 - xl, pl.ds(lo, 128)], across)

    ga = UpDown(links, place, ub, xl, 0)
    gb = UpDown(links, place, ub, xl, 128)
    gc = UpDown(links, place, ub, 1 - xl, 0)
    cross(0, 0, 0)
    gb.start()
    ga.start()
    cross(1, 0, 128)
    best[...] = jnp.full((512, 128), -1.0, F32)
    bound = limit[0]
    lane_id = lax.broadcasted_iota(jnp.int32, (1, 128), 1)
    own_first = (z * 4 + xl * 2) * 256

    def score(d, x):
        zz = (z + d + 4) % 4
        labels = lb[zz, x][0:1, :].astype(F32)
        first = (zz * 4 + x * 2 + k) * 256

        def part(r, n):
            value = lax.dot_general(units[pl.ds(r, n), :], ub[zz, x], TT, preferred_element_type=F32)
            rows = lax.broadcasted_iota(jnp.int32, (n, 128), 0) + (own_first + r)
            label = labs[pl.ds(r, n), :].astype(F32)
            top = best[pl.ds(r, n), :]
            for t in range(2):
                lanes = slice(t * 128, t * 128 + 128)
                other = lane_id + (first + t * 128)
                use = (label == labels[:, lanes]) & (other < bound) & (other != rows)
                top = jnp.maximum(top, jnp.where(use, value[:, lanes], -1.0))
            best[pl.ds(r, n), :] = top

        rows_loop(512, 256, part)

    score(0, xl)
    crossed(0, 0, 0)
    gc.start()
    gb.relay()
    cross(2, -1, 128)
    cross(3, 1, 128)
    ga.relay()
    gb.far()
    cross(4, 2, 128)

    def pair(i, carry):
        score(2 * i - 1, xl)
        return carry

    lax.fori_loop(0, 2, pair, 0)
    gc.relay()
    crossed(1, 0, 128)
    score(0, 1 - xl)
    ga.far()
    score(2, xl)
    crossed(2, -1, 128)
    crossed(3, 1, 128)

    def other_pair(i, carry):
        score(2 * i - 1, 1 - xl)
        return carry

    lax.fori_loop(0, 2, other_pair, 0)
    gc.far()
    crossed(4, 2, 128)
    score(2, 1 - xl)
    for copy in sent + ga.sent + gb.sent + gc.sent:
        copy.wait_send()
    top = jnp.max(best[...].T, axis=0, keepdims=True)
    tops[0] = jnp.broadcast_to(top, (8, 512))
    swap = links.copy(links.slot(), tops.at[0], tops.at[1], place.partner())
    swap.start()
    swap.wait()
    top = jnp.maximum(tops[0], tops[1])[0:1, :]
    out[...] = jnp.where(k == 0, top[:, 0:256], top[:, 256:512])


def whole_kernel(
    e_ref, sb_ref, s0_ref, s1_ref, ids_ref, limit, subspace, nearest, send, recv, m
):
    links, place = Links(send, recv), Place()
    k, xl = place.k, place.x % 2
    load = pltpu.make_async_copy(e_ref, m["rows"], m["rows_sem"])
    load.start()
    devices = [place.along("u", d) for d in (1, -1, 2)] + [place.partner()]
    devices += [place.in_plane(dv, dw) for dv, dw in PLANE]
    flip = 1 - 2 * xl
    devices += [place.at(flip, 0, dz, k) for dz in (1, 2, 3)]
    greet(devices)
    first_product(links, place, load, sb_ref, s0_ref, s1_ref, ids_ref, m)
    s, zs, out, ad, wp, lp = (m[n] for n in ("s", "zs", "out", "ad", "wp", "lp"))
    fill = power_step(links, place, 0, m)
    factor_apply(s, zs, CHUNKS, out, ad, wp, lp, fill)
    m["proj"][...] = out[0:512, :].astype(BF16)
    fill = power_step(links, place, 1, m)
    own_y = m["y"].at[1]
    zs[512:544, :] = own_y[:, 0:K].astype(F32) + own_y[:, K : 2 * K].astype(F32)
    factor_apply(s, zs, CHUNKS + [(512, 32)], out, ad, wp, lp, fill)
    units = m["units"]
    for i in range(4):
        coords = out[i * 128 : i * 128 + 128, :]
        size = jnp.sum(coords * coords, axis=1, keepdims=True) + EPS
        units[i * 128 : i * 128 + 128, :] = (coords * lax.rsqrt(size)).astype(BF16)
    subspace[...] = out[512:544, :] * math.sqrt(D)
    nearest_rows(links, place, limit, nearest, m)
    assert links.used <= SLOTS


def body(embeddings, start_basis, cluster_ids, valid_counts):
    s0, s1 = selections()
    vmem = pl.BlockSpec(memory_space=pltpu.VMEM)
    subspace, nearest = pl.pallas_call(
        whole_kernel,
        out_shape=[jax.ShapeDtypeStruct((32, K), F32), jax.ShapeDtypeStruct((1, 256), F32)],
        in_specs=[pl.BlockSpec(memory_space=pl.ANY)] + [vmem] * 4 + [pl.BlockSpec(memory_space=pltpu.SMEM)],
        out_specs=[vmem] * 2,
        scratch_shapes=[pltpu.SemaphoreType.DMA((SLOTS,)), pltpu.SemaphoreType.DMA((SLOTS,)), SCRATCH],
        compiler_params=pltpu.CompilerParams(
            collective_id=0, has_side_effects=True, vmem_limit_bytes=VMEM_LIMIT
        ),
        name="whole",
    )(embeddings, start_basis, s0, s1, cluster_ids.reshape(1, 256), valid_counts)
    return (subspace, nearest.reshape(256))


def solution(mesh):
    placed = (
        P(("cluster", "member"), None),
        P(("cluster", "member"), None),
        P(("cluster", "member")),
        P("cluster"),
    )
    return jax.shard_map(
        body,
        mesh=mesh,
        in_specs=placed,
        out_specs=(P(("cluster", "member"), None), P(("cluster", "member"))),
        check_vma=False,
    )
```
